512 devices in a mesh: lat: 32 (over z_hi, y), lon: 16 (over z_lo, x, core).
Axes of the slice: x: 4, y: 8, z: 8 (z_hi: 4, z_lo: 2; z = z_hi * 2 + z_lo), core: 2. Of those that a mesh axis runs over, the one named last changes fastest.
Arguments:
- obs_values: float32 [16, 2097152], P(None, ('lat', 'lon')), may hold values from -6 to 6
- obs_rows: int32 [2097152], P(('lat', 'lon')), may hold values from 0 to 95
- obs_cols: int32 [2097152], P(('lat', 'lon')), may hold values from 0 to 383
- row_frac: float32 [2097152], P(('lat', 'lon')), may hold values from 0 to 1
- col_frac: float32 [2097152], P(('lat', 'lon')), may hold values from 0 to 1
- obs_count: int32 [512], P(('lat', 'lon')), may hold values from 1 to 4096, 1572864 in all
- sigma: float32 [3072, 16, 6144], P('lat', None, 'lon'), may hold values from 0.3 to 3
- lat_scales: float32 [16], replicated, may hold values from 40 to 64
- lon_scales: float32 [16], replicated, may hold values from 40 to 64
Outputs:
- control: float32 [3072, 16, 6144], P('lat', None, 'lon')
The draws below stay inside these ranges and needn't reach their ends.
Inputs may be any that keep to these rules, and one draw needn't show every extreme that they name: Tile d (latitude tile d // 16, longitude tile d % 16) holds slots d * 4096 to (d + 1) * 4096 - 1, of which the first obs_count[d] are live; some tile has all 4096 live. `obs_rows`: counted within the observation's own tile. `obs_cols`: counted within the observation's own tile.
All inputs are finite; a program needn't handle non-finite values. No bound on the sum of `obs_count` on one device may be relied on, other than what follows from the above.
Results may differ from the reference program's by a relative error of at most 0.000098.
Values sent between devices are 32-bit elements; how exact they have to be, the bound alone decides.
A program may use at most 128 MiB of HBM per device.

```python
import math
import jax
import jax.numpy as jnp
import numpy as np
from jax import lax

ROWS = 96
COLS = 384
LEVELS = 16
OBS_DEV = 4096
HALF = 128
NLAT = 3072
NLON = 6144
N_LON = 16
DEVICES = 512


def scale_levels(key, salt):
    own_key = jax.random.fold_in(key, salt)
    uniform_part = jax.random.uniform(own_key, (LEVELS,), jnp.float32)
    lowest = 5.0 * HALF / 16.0
    highest = HALF / 2.0
    inner = jnp.exp(math.log(lowest) + uniform_part * (math.log(highest) - math.log(lowest)))
    return jnp.clip(inner, lowest, highest).astype(jnp.float32)


def draw_lat_scales(key, part):
    return scale_levels(key, 11)


def draw_lon_scales(key, part):
    return scale_levels(key, 23)


def place_ends(entries, key, smallest, high):
    dims = entries.shape
    spot = [jax.random.randint(jax.random.fold_in(key, axis), (), 0, dims[axis]) for axis in range(len(dims))]
    entries = entries.at[tuple(spot)].set(smallest)
    longest = dims.index(max(dims))
    spot[longest] = (spot[longest] + 1) % dims[longest]
    return entries.at[tuple(spot)].set(high)


def block_scale(stream_key, shape, shards, low, top_value):
    factor_of, own = 1.0, jax.random.fold_in(stream_key, 6)
    for axis_at, shards_of in shards:
        steps = jnp.exp(jax.random.uniform(jax.random.fold_in(own, axis_at), (shards_of,), jnp.float32, low / len(shards), top_value / len(shards)))
        factor_of = factor_of * jnp.repeat(steps, shape[axis_at] // shards_of).reshape([-1 if axis == axis_at else 1 for axis in range(len(shape))])
    return factor_of


def profile(number_of, total, most, slope):
    portions = [(1 << 20) // math.isqrt(grade ** slope) + 1 for grade in range(2, number_of + 1)]
    spare, given = total - most - (number_of - 1), [1] * (number_of - 1)
    while spare > 0:
        movable = [i for i in range(number_of - 1) if given[i] < most]
        mass, budget = sum([portions[i] for i in movable]), spare
        for i in movable:
            more = min(most - given[i], max(1, budget * portions[i] // mass), spare)
            given[i] = given[i] + more
            spare = spare - more
    return np.array([most] + given)


def ragged(stream_key, count, total, reach, lean):
    if count == 2:
        one = jax.random.randint(stream_key, (), max(1, total - reach), min(reach, total - 1) + 1)
        return jnp.stack([one, total - one])
    lengths = jnp.asarray(profile(count, total, reach, lean), jnp.int32)
    couples = (count - 1) // 2
    giver, taker = lengths[1:1 + 2 * couples:2], lengths[2:2 + 2 * couples:2]
    room = jnp.minimum(giver - 1, reach - taker)
    moved = jax.random.randint(jax.random.fold_in(stream_key, 1), (couples,), 0, 1 << 20) % (room + 1)
    lengths = lengths.at[1:1 + 2 * couples:2].set(giver - moved).at[2:2 + 2 * couples:2].set(taker + moved)
    return lengths[jax.random.permutation(jax.random.fold_in(stream_key, 2), count)]


def centred(rng, shape, deviation, bound, split=(), held_as=jnp.bfloat16):
    factor_of = block_scale(rng, shape, split, -0.22, 0.18) if split else 1.0
    values = jax.random.normal(rng, shape, jnp.float32) * deviation * factor_of
    return jnp.minimum(jnp.maximum(values, -bound), bound).astype(held_as)


def setup_inputs(seed: int = 0) -> dict:
    splits = jax.random.split(jax.random.key(seed), 10)
    return {
        "obs_values": centred(splits[0], (LEVELS, DEVICES * OBS_DEV), 1.0, 6.0, ((1, 512),), jnp.float32),
        "obs_rows": place_ends(jax.random.randint(splits[1], (DEVICES * OBS_DEV,), 0, ROWS), jax.random.fold_in(splits[1], 1), 0, ROWS - 1).astype(jnp.int32),
        "obs_cols": place_ends(jax.random.randint(splits[2], (DEVICES * OBS_DEV,), 0, COLS), jax.random.fold_in(splits[2], 1), 0, COLS - 1).astype(jnp.int32),
        "row_frac": jnp.clip(1.0 * jax.random.uniform(splits[3], (DEVICES * OBS_DEV,), jnp.float32) ** block_scale(splits[3], (DEVICES * OBS_DEV,), ((0, 512),), -0.2, 0.2), 0.0, 1.0),
        "col_frac": jnp.clip(1.0 * jax.random.uniform(splits[4], (DEVICES * OBS_DEV,), jnp.float32) ** block_scale(splits[4], (DEVICES * OBS_DEV,), ((0, 512),), -0.2, 0.2), 0.0, 1.0),
        "obs_count": ragged(splits[5], DEVICES, 3 * DEVICES * OBS_DEV // 4, OBS_DEV, 2).astype(jnp.int32),
        "sigma": jnp.clip(jnp.exp(math.log(3.0) - 2.3025851 * jax.random.uniform(splits[6], (NLAT, LEVELS, NLON), jnp.float32) ** block_scale(splits[6], (NLAT, LEVELS, NLON), ((0, 32), (2, 16)), -0.2, 0.2)), 0.3, 3.0),
        "lat_scales": draw_lat_scales(jax.random.fold_in(splits[9], 71), 0),
        "lon_scales": draw_lon_scales(jax.random.fold_in(splits[9], 71), 0),
    }


def kernel_matrix(scales, out_count, half_width):
    out_index = jnp.arange(out_count, dtype=jnp.int32)[:, None]
    in_index = jnp.arange(out_count + 2 * half_width, dtype=jnp.int32)[None, :]
    offset = in_index - half_width - out_index
    inside = jnp.abs(offset) <= half_width
    offset_real = offset.astype(jnp.float32)
    spread = scales.astype(jnp.float32)[:, None, None]
    tap_lag = jnp.arange(-half_width, half_width + 1, dtype=jnp.int32).astype(jnp.float32)
    energy = lax.optimization_barrier(jnp.sum(jnp.exp(-(tap_lag[None, :] * tap_lag[None, :]) / (spread[:, :, 0] * spread[:, :, 0])), axis=1))
    gaussian = jnp.exp(-(offset_real * offset_real)[None] / (2.0 * spread * spread)) / jnp.sqrt(energy)[:, None, None]
    return jnp.where(inside[None], gaussian, jnp.zeros_like(gaussian))

def reference(obs_values, obs_rows, obs_cols, row_frac, col_frac, obs_count, sigma, lat_scales, lon_scales):
    total_slots = obs_rows.shape[0]
    slot_index = jnp.arange(total_slots, dtype=jnp.int32)
    device = slot_index // OBS_DEV
    live_slot = slot_index % OBS_DEV < obs_count[device]
    base_row = device // N_LON * ROWS + obs_rows
    base_col = device % N_LON * COLS + obs_cols
    values_t = jnp.transpose(obs_values)
    scattered = jnp.zeros((NLAT * NLON, LEVELS), jnp.float32)
    for row_step in (0, 1):
        for col_step in (0, 1):
            row_weight = row_frac if row_step else 1.0 - row_frac
            col_weight = col_frac if col_step else 1.0 - col_frac
            global_row = base_row + row_step
            global_col = (base_col + col_step) % NLON
            inside_grid = live_slot & (global_row < NLAT)
            flat_index = jnp.where(inside_grid, global_row * NLON + global_col, 0).astype(jnp.int32)
            weight = jnp.where(inside_grid, row_weight * col_weight, jnp.zeros_like(row_frac))
            scattered = scattered.at[flat_index].add(values_t * weight[:, None])
    weighted = jnp.transpose(scattered.reshape(NLAT, NLON, LEVELS), (0, 2, 1)) * sigma
    block_rows = 2 * HALF
    lat_kernel = kernel_matrix(lat_scales, block_rows, HALF)
    padded = jnp.pad(weighted, ((HALF, HALF), (0, 0), (0, 0)))

    def lat_block(block_index):
        window = lax.dynamic_slice_in_dim(padded, block_index * block_rows, 2 * block_rows, 0)
        return jnp.einsum('lip,plc->ilc', lat_kernel, window, precision=lax.Precision.HIGHEST)
    lat_done = lax.map(lat_block, jnp.arange(NLAT // block_rows, dtype=jnp.int32)).reshape(NLAT, LEVELS, NLON)
    lon_kernel = kernel_matrix(lon_scales, block_rows, HALF)
    lon_blocks = NLON // block_rows

    def lon_block(block_index):
        row_slab = lax.dynamic_slice_in_dim(lat_done, block_index * block_rows, block_rows, 0)
        blocked = row_slab.reshape(block_rows, LEVELS, lon_blocks, block_rows)
        before = jnp.roll(blocked, 1, axis=2)[..., block_rows - HALF:]
        after_rim = jnp.roll(blocked, -1, axis=2)[..., :HALF]
        window = jnp.concatenate([before, blocked, after_rim], axis=3)
        result = jnp.einsum('lip,rlbp->rlbi', lon_kernel, window, precision=lax.Precision.HIGHEST)
        return result.reshape(block_rows, LEVELS, NLON)
    return lax.map(lon_block, jnp.arange(NLAT // block_rows, dtype=jnp.int32)).reshape(NLAT, LEVELS, NLON)
```

```python
import jax
import jax.numpy as jnp
from jax import lax
from jax.sharding import PartitionSpec as P

HALF = 128


def from_behind(block, axis, distance):
    devices = range(lax.axis_size(axis))
    route = [((i - distance) % len(devices), i) for i in devices]
    return lax.ppermute(block, axis, route)


def shifted(block, axis, distance):
    devices = range(lax.axis_size(axis))
    route = [(i - distance, i) for i in devices if i - distance in devices]
    return lax.ppermute(block, axis, route)


def with_halo(block, sides, width):
    for axis, dim in sides:
        count = lax.axis_size(axis)
        forward = [(i, i + 1) for i in range(count - 1)]
        forward.append((count - 1, 0))
        backward = [(target, source) for source, target in forward]
        low = lax.ppermute(
            lax.slice_in_dim(block, block.shape[dim] - width, None, axis=dim), axis, forward
        )
        high = lax.ppermute(lax.slice_in_dim(block, 0, width, axis=dim), axis, backward)
        block = jnp.concatenate([low, block, high], axis=dim)
    return block


def kernel_matrix(scales, out_count, half_width):
    out_index = jnp.arange(out_count, dtype=jnp.int32)[:, None]
    in_index = jnp.arange(out_count + 2 * half_width, dtype=jnp.int32)[None, :]
    offset = in_index - half_width - out_index
    inside = jnp.abs(offset) <= half_width
    offset_real = offset.astype(jnp.float32)
    spread = scales[:, None, None]
    tap_lag = jnp.arange(-half_width, half_width + 1, dtype=jnp.int32).astype(jnp.float32)
    energy = jnp.sum(
        jnp.exp(-(tap_lag[None, :] * tap_lag[None, :]) / (spread[:, :, 0] * spread[:, :, 0])),
        axis=1,
    )
    gaussian = (
        jnp.exp(-(offset_real * offset_real)[None] / (2.0 * spread * spread))
        / jnp.sqrt(energy)[:, None, None]
    )
    return jnp.where(inside[None], gaussian, jnp.zeros_like(gaussian))


def corner_weights(index, frac, count):
    cells = jnp.arange(count, dtype=jnp.int32)[None, :]
    low = jnp.where(cells == index[:, None], (1.0 - frac)[:, None], 0.0)
    high = jnp.where(cells == index[:, None] + 1, frac[:, None], 0.0)
    return low + high


def lat_halo(block, width):
    rows = block.shape[0]
    parts = []
    reach = width
    distance = 1
    below, above = [], []
    while reach > 0:
        take = min(rows, reach)
        below.insert(0, shifted(block[rows - take :], "lat", distance))
        above.append(shifted(block[:take], "lat", -distance))
        reach -= take
        distance += 1
    parts = below + [block] + above
    return jnp.concatenate(parts, axis=0)


def shards(
    obs_values, obs_rows, obs_cols, row_frac, col_frac, obs_count, sigma, lat_scales, lon_scales
):
    tile_rows, level_count, tile_cols = sigma.shape
    slot_total = obs_rows.shape[0]
    live_slot = jnp.arange(slot_total, dtype=jnp.int32) < obs_count[0]
    values_t = jnp.where(live_slot[:, None], jnp.transpose(obs_values), 0.0)
    row_w = corner_weights(obs_rows, row_frac, tile_rows + 1)
    col_w = corner_weights(obs_cols, col_frac, tile_cols + 1)
    row_values = row_w[:, :, None] * values_t[:, None, :]
    extended = jnp.einsum(
        "krl,kc->rlc", row_values, col_w, precision=lax.Precision.HIGH
    )
    edge_column = from_behind(extended[:, :, tile_cols], "lon", 1)
    folded = extended[:, :, :tile_cols].at[:, :, 0].add(edge_column)
    edge_row = shifted(folded[tile_rows], "lat", 1)
    weighted = folded[:tile_rows].at[0].add(edge_row) * sigma
    half_width = HALF
    window = lat_halo(weighted, half_width)
    lat_kernel = kernel_matrix(lat_scales, tile_rows, half_width)
    lat_done = jnp.einsum(
        "lip,plc->ilc", lat_kernel, window, precision=lax.Precision.HIGHEST
    )
    padded_cols = with_halo(lat_done, (("lon", 2),), half_width)
    lon_kernel = kernel_matrix(lon_scales, tile_cols, half_width)
    result = jnp.einsum("lip,rlp->rli", lon_kernel, padded_cols, precision=lax.Precision.HIGHEST)
    return result


def solution(mesh):
    in_specs = (
        P(None, ("lat", "lon")),
        P(("lat", "lon")),
        P(("lat", "lon")),
        P(("lat", "lon")),
        P(("lat", "lon")),
        P(("lat", "lon")),
        P("lat", None, "lon"),
        P(),
        P(),
    )
    out_specs = P("lat", None, "lon")
    return jax.shard_map(shards, mesh=mesh, in_specs=in_specs, out_specs=out_specs, check_vma=False)
```

```python
import functools

import jax
import jax.numpy as jnp
from jax import lax
from jax.sharding import PartitionSpec as P

HALF = 128


def from_behind(block, axis, distance):
    devices = range(lax.axis_size(axis))
    route = [((i - distance) % len(devices), i) for i in devices]
    return lax.ppermute(block, axis, route)


def shifted(block, axis, distance):
    devices = range(lax.axis_size(axis))
    route = [(i - distance, i) for i in devices if i - distance in devices]
    return lax.ppermute(block, axis, route)


def with_halo(block, sides, width):
    for axis, dim in sides:
        count = lax.axis_size(axis)
        forward = [(i, i + 1) for i in range(count - 1)]
        forward.append((count - 1, 0))
        backward = [(target, source) for source, target in forward]
        low = lax.ppermute(
            lax.slice_in_dim(block, block.shape[dim] - width, None, axis=dim), axis, forward
        )
        high = lax.ppermute(lax.slice_in_dim(block, 0, width, axis=dim), axis, backward)
        block = jnp.concatenate([low, block, high], axis=dim)
    return block


def kernel_matrix(scales, out_count, half_width):
    out_index = jnp.arange(out_count, dtype=jnp.int32)[:, None]
    in_index = jnp.arange(out_count + 2 * half_width, dtype=jnp.int32)[None, :]
    offset = in_index - half_width - out_index
    inside = jnp.abs(offset) <= half_width
    offset_real = offset.astype(jnp.float32)
    spread = scales[:, None, None]
    tap_lag = jnp.arange(-half_width, half_width + 1, dtype=jnp.int32).astype(jnp.float32)
    energy = jnp.sum(
        jnp.exp(-(tap_lag[None, :] * tap_lag[None, :]) / (spread[:, :, 0] * spread[:, :, 0])),
        axis=1,
    )
    gaussian = (
        jnp.exp(-(offset_real * offset_real)[None] / (2.0 * spread * spread))
        / jnp.sqrt(energy)[:, None, None]
    )
    return jnp.where(inside[None], gaussian, jnp.zeros_like(gaussian))


def corner_weights(index, frac, count):
    cells = jnp.arange(count, dtype=jnp.int32)[None, :]
    low = jnp.where(cells == index[:, None], (1.0 - frac)[:, None], 0.0)
    high = jnp.where(cells == index[:, None] + 1, frac[:, None], 0.0)
    return low + high


def lat_move(block, pairs):
    if not pairs:
        return jnp.zeros_like(block)
    return lax.ppermute(block, "lat", pairs)


def lat_shift(block, distance, groups):
    count = len(groups)
    step = 1 if distance > 0 else -1
    pairs = [(s, s + distance) for s in range(count) if 0 <= s + distance < count]
    direct = [(s, t) for s, t in pairs if groups[s] == groups[t]]
    cross = [(s, t) for s, t in pairs if groups[s] != groups[t]]
    received = lat_move(block, direct)
    if not cross:
        return received
    span = 0
    while groups[span] == groups[0]:
        span += 1
    half = block.shape[1] // 2
    first, second = block[:, :half], block[:, half:]
    via_a = [(s, s + step * span) for s, t in cross]
    via_b = [(s, t - step * span) for s, t in cross]
    moved_a = lat_move(lat_move(first, via_a), [(r, t) for (s, r), (_, t) in zip(via_a, cross)])
    moved_b = lat_move(lat_move(second, via_b), [(r, t) for (s, r), (_, t) in zip(via_b, cross)])
    return received + jnp.concatenate([moved_a, moved_b], axis=1)


def lat_halo(block, width, groups):
    rows = block.shape[0]
    reach = width
    distance = 1
    below, above = [], []
    while reach > 0:
        take = min(rows, reach)
        below.insert(0, lat_shift(block[rows - take :], distance, groups))
        above.append(lat_shift(block[:take], -distance, groups))
        reach -= take
        distance += 1
    return jnp.concatenate(below + [block] + above, axis=0)


def shards(
    groups,
    obs_values, obs_rows, obs_cols, row_frac, col_frac, obs_count, sigma, lat_scales, lon_scales
):
    tile_rows, level_count, tile_cols = sigma.shape
    slot_total = obs_rows.shape[0]
    live_slot = jnp.arange(slot_total, dtype=jnp.int32) < obs_count[0]
    values_t = jnp.where(live_slot[:, None], jnp.transpose(obs_values), 0.0)
    row_w = corner_weights(obs_rows, row_frac, tile_rows + 1)
    col_w = corner_weights(obs_cols, col_frac, tile_cols + 1)
    row_values = row_w[:, :, None] * values_t[:, None, :]
    extended = jnp.einsum(
        "krl,kc->rlc", row_values, col_w, precision=lax.Precision.HIGH
    )
    edge_column = from_behind(extended[:, :, tile_cols], "lon", 1)
    folded = extended[:, :, :tile_cols].at[:, :, 0].add(edge_column)
    edge_row = shifted(folded[tile_rows], "lat", 1)
    weighted = folded[:tile_rows].at[0].add(edge_row) * sigma
    half_width = HALF
    window = lat_halo(weighted, half_width, groups)
    lat_kernel = kernel_matrix(lat_scales, tile_rows, half_width)
    lat_done = jnp.einsum(
        "lip,plc->ilc", lat_kernel, window, precision=lax.Precision.HIGHEST
    )
    padded_cols = with_halo(lat_done, (("lon", 2),), half_width)
    lon_kernel = kernel_matrix(lon_scales, tile_cols, half_width)
    result = jnp.einsum("lip,rlp->rli", lon_kernel, padded_cols, precision=lax.Precision.HIGHEST)
    return result


def lat_groups(mesh):
    column = mesh.devices[:, 0]
    coords = [getattr(device, "coords", None) for device in column]
    if any(c is None for c in coords):
        return tuple(index // 8 for index in range(len(column)))
    return tuple(c[2] // 2 for c in coords)


def solution(mesh):
    in_specs = (
        P(None, ("lat", "lon")),
        P(("lat", "lon")),
        P(("lat", "lon")),
        P(("lat", "lon")),
        P(("lat", "lon")),
        P(("lat", "lon")),
        P("lat", None, "lon"),
        P(),
        P(),
    )
    out_specs = P("lat", None, "lon")
    groups = lat_groups(mesh)
    return jax.shard_map(functools.partial(shards, groups), mesh=mesh, in_specs=in_specs, out_specs=out_specs, check_vma=False)
```

```python
import functools

import jax
import jax.numpy as jnp
from jax import lax
from jax.sharding import PartitionSpec as P

HALF = 128


def from_behind(block, axis, distance):
    devices = range(lax.axis_size(axis))
    route = [((i - distance) % len(devices), i) for i in devices]
    return lax.ppermute(block, axis, route)


def shifted(block, axis, distance):
    devices = range(lax.axis_size(axis))
    route = [(i - distance, i) for i in devices if i - distance in devices]
    return lax.ppermute(block, axis, route)


def with_halo(block, sides, width):
    for axis, dim in sides:
        count = lax.axis_size(axis)
        forward = [(i, i + 1) for i in range(count - 1)]
        forward.append((count - 1, 0))
        backward = [(target, source) for source, target in forward]
        low = lax.ppermute(
            lax.slice_in_dim(block, block.shape[dim] - width, None, axis=dim), axis, forward
        )
        high = lax.ppermute(lax.slice_in_dim(block, 0, width, axis=dim), axis, backward)
        block = jnp.concatenate([low, block, high], axis=dim)
    return block


def kernel_matrix(scales, out_count, half_width):
    out_index = jnp.arange(out_count, dtype=jnp.int32)[:, None]
    in_index = jnp.arange(out_count + 2 * half_width, dtype=jnp.int32)[None, :]
    offset = in_index - half_width - out_index
    inside = jnp.abs(offset) <= half_width
    offset_real = offset.astype(jnp.float32)
    spread = scales[:, None, None]
    tap_lag = jnp.arange(-half_width, half_width + 1, dtype=jnp.int32).astype(jnp.float32)
    energy = jnp.sum(
        jnp.exp(-(tap_lag[None, :] * tap_lag[None, :]) / (spread[:, :, 0] * spread[:, :, 0])),
        axis=1,
    )
    gaussian = (
        jnp.exp(-(offset_real * offset_real)[None] / (2.0 * spread * spread))
        / jnp.sqrt(energy)[:, None, None]
    )
    return jnp.where(inside[None], gaussian, jnp.zeros_like(gaussian))


def corner_weights(index, frac, count):
    cells = jnp.arange(count, dtype=jnp.int32)[None, :]
    low = jnp.where(cells == index[:, None], (1.0 - frac)[:, None], 0.0)
    high = jnp.where(cells == index[:, None] + 1, frac[:, None], 0.0)
    return low + high


def lat_move(block, pairs):
    if not pairs:
        return jnp.zeros_like(block)
    return lax.ppermute(block, "lat", pairs)


def lat_shift(block, distance, groups):
    count = len(groups)
    pairs = [(s, s + distance) for s in range(count) if 0 <= s + distance < count]
    cross = [(s, t) for s, t in pairs if groups[s] != groups[t]]
    if abs(distance) != 1 or not cross:
        return lat_move(block, pairs)
    span = groups.index(groups[0] + 1)
    step = 1 if distance > 0 else -1
    relays = [(s, t - step * span) for s, t in cross]
    first_pairs = [(s, t) for s, t in pairs if (s, t) not in cross] + relays
    half = block.shape[1] // 2
    direct = lat_move(block[:, :half], pairs)
    staged = lat_move(block[:, half:], first_pairs)
    forwarded = lat_move(staged, [(r, t) for (s, r), (_, t) in zip(relays, cross)])
    here = lax.axis_index("lat")
    targets = [t for s, t in cross]
    relay_only = [r for s, r in relays if r not in targets]
    is_target = jnp.isin(here, jnp.array(targets, jnp.int32))
    is_relay = jnp.isin(here, jnp.array(relay_only, jnp.int32))
    second = jnp.where(is_target, forwarded, jnp.where(is_relay, 0.0, staged))
    return jnp.concatenate([direct, second], axis=1)


def lat_halo(block, width, groups):
    rows = block.shape[0]
    reach = width
    distance = 1
    below, above = [], []
    while reach > 0:
        take = min(rows, reach)
        below.insert(0, lat_shift(block[rows - take :], distance, groups))
        above.append(lat_shift(block[:take], -distance, groups))
        reach -= take
        distance += 1
    return jnp.concatenate(below + [block] + above, axis=0)


def shards(
    groups,
    obs_values, obs_rows, obs_cols, row_frac, col_frac, obs_count, sigma, lat_scales, lon_scales
):
    tile_rows, level_count, tile_cols = sigma.shape
    slot_total = obs_rows.shape[0]
    live_slot = jnp.arange(slot_total, dtype=jnp.int32) < obs_count[0]
    values_t = jnp.where(live_slot[:, None], jnp.transpose(obs_values), 0.0)
    row_w = corner_weights(obs_rows, row_frac, tile_rows + 1)
    col_w = corner_weights(obs_cols, col_frac, tile_cols + 1)
    row_values = row_w[:, :, None] * values_t[:, None, :]
    extended = jnp.einsum(
        "krl,kc->rlc", row_values, col_w, precision=lax.Precision.HIGH
    )
    edge_column = from_behind(extended[:, :, tile_cols], "lon", 1)
    folded = jnp.concatenate(
        [(extended[:, :, 0] + edge_column)[:, :, None], extended[:, :, 1:tile_cols]], axis=2
    )
    edge_row = shifted(folded[tile_rows], "lat", 1)
    departures = jnp.concatenate([(folded[0] + edge_row)[None], folded[1:tile_rows]], axis=0)
    weighted = departures * sigma
    half_width = HALF
    window = lat_halo(weighted, half_width, groups)
    lat_kernel = kernel_matrix(lat_scales, tile_rows, half_width)
    lat_done = jnp.einsum(
        "lip,plc->ilc", lat_kernel, window, precision=lax.Precision.HIGHEST
    )
    padded_cols = with_halo(lat_done, (("lon", 2),), half_width)
    lon_kernel = kernel_matrix(lon_scales, tile_cols, half_width)
    result = jnp.einsum("lip,rlp->rli", lon_kernel, padded_cols, precision=lax.Precision.HIGHEST)
    return result


def lat_groups(mesh):
    column = mesh.devices[:, 0]
    coords = [getattr(device, "coords", None) for device in column]
    if any(c is None for c in coords):
        return tuple(index // 8 for index in range(len(column)))
    return tuple(c[2] // 2 for c in coords)


def solution(mesh):
    in_specs = (
        P(None, ("lat", "lon")),
        P(("lat", "lon")),
        P(("lat", "lon")),
        P(("lat", "lon")),
        P(("lat", "lon")),
        P(("lat", "lon")),
        P("lat", None, "lon"),
        P(),
        P(),
    )
    out_specs = P("lat", None, "lon")
    groups = lat_groups(mesh)
    return jax.shard_map(functools.partial(shards, groups), mesh=mesh, in_specs=in_specs, out_specs=out_specs, check_vma=False)
```

```python
import jax
import jax.numpy as jnp
from jax import lax
from jax.sharding import PartitionSpec as P

HALF = 128


def from_behind(block, axis, distance):
    devices = range(lax.axis_size(axis))
    route = [((i - distance) % len(devices), i) for i in devices]
    return lax.ppermute(block, axis, route)


def shifted(block, axis, distance):
    devices = range(lax.axis_size(axis))
    route = [(i - distance, i) for i in devices if i - distance in devices]
    return lax.ppermute(block, axis, route)


def with_halo(block, sides, width):
    for axis, dim in sides:
        count = lax.axis_size(axis)
        forward = [(i, i + 1) for i in range(count - 1)]
        forward.append((count - 1, 0))
        backward = [(target, source) for source, target in forward]
        low = lax.ppermute(
            lax.slice_in_dim(block, block.shape[dim] - width, None, axis=dim), axis, forward
        )
        high = lax.ppermute(lax.slice_in_dim(block, 0, width, axis=dim), axis, backward)
        block = jnp.concatenate([low, block, high], axis=dim)
    return block


def kernel_matrix(scales, out_count, half_width):
    out_index = jnp.arange(out_count, dtype=jnp.int32)[:, None]
    in_index = jnp.arange(out_count + 2 * half_width, dtype=jnp.int32)[None, :]
    offset = in_index - half_width - out_index
    inside = jnp.abs(offset) <= half_width
    offset_real = offset.astype(jnp.float32)
    spread = scales[:, None, None]
    tap_lag = jnp.arange(-half_width, half_width + 1, dtype=jnp.int32).astype(jnp.float32)
    energy = jnp.sum(
        jnp.exp(-(tap_lag[None, :] * tap_lag[None, :]) / (spread[:, :, 0] * spread[:, :, 0])),
        axis=1,
    )
    gaussian = (
        jnp.exp(-(offset_real * offset_real)[None] / (2.0 * spread * spread))
        / jnp.sqrt(energy)[:, None, None]
    )
    return jnp.where(inside[None], gaussian, jnp.zeros_like(gaussian))


def corner_weights(index, frac, count):
    cells = jnp.arange(count, dtype=jnp.int32)[None, :]
    low = jnp.where(cells == index[:, None], (1.0 - frac)[:, None], 0.0)
    high = jnp.where(cells == index[:, None] + 1, frac[:, None], 0.0)
    return low + high


def lat_halo(block, width):
    rows = block.shape[0]
    parts = []
    reach = width
    distance = 1
    below, above = [], []
    while reach > 0:
        take = min(rows, reach)
        below.insert(0, shifted(block[rows - take :], "lat", distance))
        above.append(shifted(block[:take], "lat", -distance))
        reach -= take
        distance += 1
    parts = below + [block] + above
    return jnp.concatenate(parts, axis=0)


def shards(
    obs_values, obs_rows, obs_cols, row_frac, col_frac, obs_count, sigma, lat_scales, lon_scales
):
    tile_rows, level_count, tile_cols = sigma.shape
    slot_total = obs_rows.shape[0]
    live_slot = jnp.arange(slot_total, dtype=jnp.int32) < obs_count[0]
    values_t = jnp.where(live_slot[:, None], jnp.transpose(obs_values), 0.0)
    row_w = corner_weights(obs_rows, row_frac, tile_rows + 1)
    col_w = corner_weights(obs_cols, col_frac, tile_cols + 1)
    row_values = row_w[:, :, None] * values_t[:, None, :]
    extended = jnp.einsum(
        "krl,kc->rlc", row_values, col_w, precision=lax.Precision.HIGH
    )
    edge_column = from_behind(extended[:, :, tile_cols], "lon", 1)
    folded = jnp.concatenate(
        [(extended[:, :, 0] + edge_column)[:, :, None], extended[:, :, 1:tile_cols]], axis=2
    )
    edge_row = shifted(folded[tile_rows], "lat", 1)
    departures = jnp.concatenate([(folded[0] + edge_row)[None], folded[1:tile_rows]], axis=0)
    weighted = departures * sigma
    half_width = HALF
    window = lat_halo(weighted, half_width)
    lat_kernel = kernel_matrix(lat_scales, tile_rows, half_width)
    lat_done = jnp.einsum(
        "lip,plc->ilc", lat_kernel, window, precision=lax.Precision.HIGH
    )
    padded_cols = with_halo(lat_done, (("lon", 2),), half_width)
    band = half_width
    lon_kernel = kernel_matrix(lon_scales, band, half_width)
    band_count = tile_cols // band
    bands = jnp.stack(
        [padded_cols[:, :, b * band : b * band + band + 2 * half_width] for b in range(band_count)],
        axis=2,
    )
    result = jnp.einsum("lip,rlbp->rlbi", lon_kernel, bands, precision=lax.Precision.HIGH)
    return result.reshape(tile_rows, level_count, tile_cols)


def solution(mesh):
    in_specs = (
        P(None, ("lat", "lon")),
        P(("lat", "lon")),
        P(("lat", "lon")),
        P(("lat", "lon")),
        P(("lat", "lon")),
        P(("lat", "lon")),
        P("lat", None, "lon"),
        P(),
        P(),
    )
    out_specs = P("lat", None, "lon")
    return jax.shard_map(shards, mesh=mesh, in_specs=in_specs, out_specs=out_specs, check_vma=False)
```

```python
import jax
import jax.numpy as jnp
from jax import lax
from jax.sharding import PartitionSpec as P

HALF = 128


def from_behind(block, axis, distance):
    devices = range(lax.axis_size(axis))
    route = [((i - distance) % len(devices), i) for i in devices]
    return lax.ppermute(block, axis, route)


def shifted(block, axis, distance):
    devices = range(lax.axis_size(axis))
    route = [(i - distance, i) for i in devices if i - distance in devices]
    return lax.ppermute(block, axis, route)


def with_halo(block, sides, width):
    for axis, dim in sides:
        count = lax.axis_size(axis)
        forward = [(i, i + 1) for i in range(count - 1)]
        forward.append((count - 1, 0))
        backward = [(target, source) for source, target in forward]
        low = lax.ppermute(
            lax.slice_in_dim(block, block.shape[dim] - width, None, axis=dim), axis, forward
        )
        high = lax.ppermute(lax.slice_in_dim(block, 0, width, axis=dim), axis, backward)
        block = jnp.concatenate([low, block, high], axis=dim)
    return block


def kernel_matrix(scales, out_count, half_width):
    out_index = jnp.arange(out_count, dtype=jnp.int32)[:, None]
    in_index = jnp.arange(out_count + 2 * half_width, dtype=jnp.int32)[None, :]
    offset = in_index - half_width - out_index
    inside = jnp.abs(offset) <= half_width
    offset_real = offset.astype(jnp.float32)
    spread = scales[:, None, None]
    tap_lag = jnp.arange(-half_width, half_width + 1, dtype=jnp.int32).astype(jnp.float32)
    energy = jnp.sum(
        jnp.exp(-(tap_lag[None, :] * tap_lag[None, :]) / (spread[:, :, 0] * spread[:, :, 0])),
        axis=1,
    )
    gaussian = (
        jnp.exp(-(offset_real * offset_real)[None] / (2.0 * spread * spread))
        / jnp.sqrt(energy)[:, None, None]
    )
    return jnp.where(inside[None], gaussian, jnp.zeros_like(gaussian))


def corner_weights(index, frac, count):
    cells = jnp.arange(count, dtype=jnp.int32)[None, :]
    low = jnp.where(cells == index[:, None], (1.0 - frac)[:, None], 0.0)
    high = jnp.where(cells == index[:, None] + 1, frac[:, None], 0.0)
    return low + high


def lat_halo(block, width):
    rows = block.shape[0]
    parts = []
    reach = width
    distance = 1
    below, above = [], []
    while reach > 0:
        take = min(rows, reach)
        below.insert(0, shifted(block[rows - take :], "lat", distance))
        above.append(shifted(block[:take], "lat", -distance))
        reach -= take
        distance += 1
    parts = below + [block] + above
    return jnp.concatenate(parts, axis=0)


def shards(
    obs_values, obs_rows, obs_cols, row_frac, col_frac, obs_count, sigma, lat_scales, lon_scales
):
    chunks = 2
    size = sigma.shape[1] // chunks
    pieces = [
        chain(
            obs_values[c * size : (c + 1) * size],
            obs_rows,
            obs_cols,
            row_frac,
            col_frac,
            obs_count,
            sigma[:, c * size : (c + 1) * size],
            lat_scales[c * size : (c + 1) * size],
            lon_scales[c * size : (c + 1) * size],
        )
        for c in range(chunks)
    ]
    return jnp.concatenate(pieces, axis=1)


def chain(
    obs_values, obs_rows, obs_cols, row_frac, col_frac, obs_count, sigma, lat_scales, lon_scales
):
    tile_rows, level_count, tile_cols = sigma.shape
    slot_total = obs_rows.shape[0]
    live_slot = jnp.arange(slot_total, dtype=jnp.int32) < obs_count[0]
    values_t = jnp.where(live_slot[:, None], jnp.transpose(obs_values), 0.0)
    row_w = corner_weights(obs_rows, row_frac, tile_rows + 1)
    col_w = corner_weights(obs_cols, col_frac, tile_cols + 1)
    row_values = row_w[:, :, None] * values_t[:, None, :]
    extended = jnp.einsum(
        "krl,kc->rlc", row_values, col_w, precision=lax.Precision.HIGH
    )
    edge_column = from_behind(extended[:, :, tile_cols], "lon", 1)
    folded = jnp.concatenate(
        [(extended[:, :, 0] + edge_column)[:, :, None], extended[:, :, 1:tile_cols]], axis=2
    )
    edge_row = shifted(folded[tile_rows], "lat", 1)
    departures = jnp.concatenate([(folded[0] + edge_row)[None], folded[1:tile_rows]], axis=0)
    weighted = departures * sigma
    half_width = HALF
    window = lat_halo(weighted, half_width)
    lat_kernel = kernel_matrix(lat_scales, tile_rows, half_width)
    lat_done = jnp.einsum(
        "lip,plc->ilc", lat_kernel, window, precision=lax.Precision.HIGH
    )
    padded_cols = with_halo(lat_done, (("lon", 2),), half_width)
    band = half_width
    lon_kernel = kernel_matrix(lon_scales, band, half_width)
    band_count = tile_cols // band
    bands = jnp.stack(
        [padded_cols[:, :, b * band : b * band + band + 2 * half_width] for b in range(band_count)],
        axis=2,
    )
    result = jnp.einsum("lip,rlbp->rlbi", lon_kernel, bands, precision=lax.Precision.HIGH)
    return result.reshape(tile_rows, level_count, tile_cols)


def solution(mesh):
    in_specs = (
        P(None, ("lat", "lon")),
        P(("lat", "lon")),
        P(("lat", "lon")),
        P(("lat", "lon")),
        P(("lat", "lon")),
        P(("lat", "lon")),
        P("lat", None, "lon"),
        P(),
        P(),
    )
    out_specs = P("lat", None, "lon")
    return jax.shard_map(shards, mesh=mesh, in_specs=in_specs, out_specs=out_specs, check_vma=False)
```

```python
import functools

import jax
import jax.numpy as jnp
from jax import lax
from jax.experimental import pallas as pl
from jax.experimental.pallas import tpu as pltpu
from jax.sharding import PartitionSpec as P

HALF = 128


def from_behind(block, axis, distance):
    devices = range(lax.axis_size(axis))
    route = [((i - distance) % len(devices), i) for i in devices]
    return lax.ppermute(block, axis, route)


def shifted(block, axis, distance):
    devices = range(lax.axis_size(axis))
    route = [(i - distance, i) for i in devices if i - distance in devices]
    return lax.ppermute(block, axis, route)


def with_halo(block, sides, width):
    for axis, dim in sides:
        count = lax.axis_size(axis)
        forward = [(i, i + 1) for i in range(count - 1)]
        forward.append((count - 1, 0))
        backward = [(target, source) for source, target in forward]
        low = lax.ppermute(
            lax.slice_in_dim(block, block.shape[dim] - width, None, axis=dim), axis, forward
        )
        high = lax.ppermute(lax.slice_in_dim(block, 0, width, axis=dim), axis, backward)
        block = jnp.concatenate([low, block, high], axis=dim)
    return block


def kernel_matrix(scales, out_count, half_width):
    out_index = jnp.arange(out_count, dtype=jnp.int32)[:, None]
    in_index = jnp.arange(out_count + 2 * half_width, dtype=jnp.int32)[None, :]
    offset = in_index - half_width - out_index
    inside = jnp.abs(offset) <= half_width
    offset_real = offset.astype(jnp.float32)
    spread = scales[:, None, None]
    tap_lag = jnp.arange(-half_width, half_width + 1, dtype=jnp.int32).astype(jnp.float32)
    energy = jnp.sum(
        jnp.exp(-(tap_lag[None, :] * tap_lag[None, :]) / (spread[:, :, 0] * spread[:, :, 0])),
        axis=1,
    )
    gaussian = (
        jnp.exp(-(offset_real * offset_real)[None] / (2.0 * spread * spread))
        / jnp.sqrt(energy)[:, None, None]
    )
    return jnp.where(inside[None], gaussian, jnp.zeros_like(gaussian))


def corner_weights(index, frac, count):
    cells = jnp.arange(count, dtype=jnp.int32)[None, :]
    low = jnp.where(cells == index[:, None], (1.0 - frac)[:, None], 0.0)
    high = jnp.where(cells == index[:, None] + 1, frac[:, None], 0.0)
    return low + high


def lat_halo(block, width):
    rows = block.shape[0]
    parts = []
    reach = width
    distance = 1
    below, above = [], []
    while reach > 0:
        take = min(rows, reach)
        below.insert(0, shifted(block[rows - take :], "lat", distance))
        above.append(shifted(block[:take], "lat", -distance))
        reach -= take
        distance += 1
    parts = below + [block] + above
    return jnp.concatenate(parts, axis=0)


def halo_body(count, rows, far, x_ref, below_ref, above_ref, send_sem, recv_sem):
    here = lax.axis_index("lat")
    column = lax.axis_index("lon")
    mesh = pl.DeviceIdType.MESH
    barrier = pltpu.get_barrier_semaphore()
    partners = ((1, 0), (2, 1), (-1, 2), (-2, 3))
    for step, slot in partners:
        neighbour = lax.rem(here + step + count, count)
        pl.semaphore_signal(barrier, 1, device_id=(neighbour, column), device_id_type=mesh)
    pl.semaphore_wait(barrier, len(partners))

    def copy(step, slot, device):
        if step == 1:
            src, dst = x_ref, below_ref.at[pl.ds(far, rows)]
        elif step == 2:
            src, dst = x_ref.at[pl.ds(rows - far, far)], below_ref.at[pl.ds(0, far)]
        elif step == -1:
            src, dst = x_ref, above_ref.at[pl.ds(0, rows)]
        else:
            src, dst = x_ref.at[pl.ds(0, far)], above_ref.at[pl.ds(rows, far)]
        return pltpu.make_async_remote_copy(
            src_ref=src, dst_ref=dst, send_sem=send_sem.at[slot], recv_sem=recv_sem.at[slot],
            device_id=(device, column), device_id_type=mesh,
        )

    for step, slot in partners:
        @pl.when(jnp.logical_and(here + step >= 0, here + step < count))
        def _():
            copy(step, slot, here + step).start()
    for step, slot in partners:
        @pl.when(jnp.logical_and(here + step >= 0, here + step < count))
        def _():
            copy(step, slot, here + step).wait_send()
        @pl.when(jnp.logical_and(here - step >= 0, here - step < count))
        def _():
            copy(step, slot, here - step).wait_recv()


def lat_halo_kernel(block, width):
    rows = block.shape[0]
    far = width - rows
    count = lax.axis_size("lat")
    halo_shape = jax.ShapeDtypeStruct((width,) + block.shape[1:], block.dtype)
    below, above = pl.pallas_call(
        functools.partial(halo_body, count, rows, far),
        out_shape=(halo_shape, halo_shape),
        in_specs=[pl.BlockSpec(memory_space=pl.ANY)],
        out_specs=(pl.BlockSpec(memory_space=pl.ANY), pl.BlockSpec(memory_space=pl.ANY)),
        scratch_shapes=[pltpu.SemaphoreType.DMA((4,)), pltpu.SemaphoreType.DMA((4,))],
        compiler_params=pltpu.CompilerParams(collective_id=0, has_side_effects=True),
    )(block)
    here = lax.axis_index("lat")
    row = jnp.arange(width)[:, None, None]
    below = jnp.where(jnp.where(row >= far, here >= 1, here >= 2), below, 0.0)
    above = jnp.where(jnp.where(row < rows, here + 1 < count, here + 2 < count), above, 0.0)
    return jnp.concatenate([below, block, above], axis=0)


def shards(
    obs_values, obs_rows, obs_cols, row_frac, col_frac, obs_count, sigma, lat_scales, lon_scales
):
    tile_rows, level_count, tile_cols = sigma.shape
    slot_total = obs_rows.shape[0]
    live_slot = jnp.arange(slot_total, dtype=jnp.int32) < obs_count[0]
    values_t = jnp.where(live_slot[:, None], jnp.transpose(obs_values), 0.0)
    row_w = corner_weights(obs_rows, row_frac, tile_rows + 1)
    col_w = corner_weights(obs_cols, col_frac, tile_cols + 1)
    row_values = row_w[:, :, None] * values_t[:, None, :]
    extended = jnp.einsum(
        "krl,kc->rlc", row_values, col_w, precision=lax.Precision.HIGH
    )
    edge_column = from_behind(extended[:, :, tile_cols], "lon", 1)
    folded = jnp.concatenate(
        [(extended[:, :, 0] + edge_column)[:, :, None], extended[:, :, 1:tile_cols]], axis=2
    )
    edge_row = shifted(folded[tile_rows], "lat", 1)
    departures = jnp.concatenate([(folded[0] + edge_row)[None], folded[1:tile_rows]], axis=0)
    weighted = departures * sigma
    half_width = HALF
    window = lat_halo_kernel(weighted, half_width)
    lat_kernel = kernel_matrix(lat_scales, tile_rows, half_width)
    lat_done = jnp.einsum(
        "lip,plc->ilc", lat_kernel, window, precision=lax.Precision.HIGH
    )
    padded_cols = with_halo(lat_done, (("lon", 2),), half_width)
    band = half_width
    lon_kernel = kernel_matrix(lon_scales, band, half_width)
    band_count = tile_cols // band
    bands = jnp.stack(
        [padded_cols[:, :, b * band : b * band + band + 2 * half_width] for b in range(band_count)],
        axis=2,
    )
    result = jnp.einsum("lip,rlbp->rlbi", lon_kernel, bands, precision=lax.Precision.HIGH)
    return result.reshape(tile_rows, level_count, tile_cols)


def solution(mesh):
    in_specs = (
        P(None, ("lat", "lon")),
        P(("lat", "lon")),
        P(("lat", "lon")),
        P(("lat", "lon")),
        P(("lat", "lon")),
        P(("lat", "lon")),
        P("lat", None, "lon"),
        P(),
        P(),
    )
    out_specs = P("lat", None, "lon")
    return jax.shard_map(shards, mesh=mesh, in_specs=in_specs, out_specs=out_specs, check_vma=False)
```

```python
import functools

import jax
import jax.numpy as jnp
from jax import lax
from jax.experimental import pallas as pl
from jax.experimental.pallas import tpu as pltpu
from jax.sharding import PartitionSpec as P

HALF = 128


def from_behind(block, axis, distance):
    devices = range(lax.axis_size(axis))
    route = [((i - distance) % len(devices), i) for i in devices]
    return lax.ppermute(block, axis, route)


def shifted(block, axis, distance):
    devices = range(lax.axis_size(axis))
    route = [(i - distance, i) for i in devices if i - distance in devices]
    return lax.ppermute(block, axis, route)


def with_halo(block, sides, width):
    for axis, dim in sides:
        count = lax.axis_size(axis)
        forward = [(i, i + 1) for i in range(count - 1)]
        forward.append((count - 1, 0))
        backward = [(target, source) for source, target in forward]
        low = lax.ppermute(
            lax.slice_in_dim(block, block.shape[dim] - width, None, axis=dim), axis, forward
        )
        high = lax.ppermute(lax.slice_in_dim(block, 0, width, axis=dim), axis, backward)
        block = jnp.concatenate([low, block, high], axis=dim)
    return block


def kernel_matrix(scales, out_count, half_width):
    out_index = jnp.arange(out_count, dtype=jnp.int32)[:, None]
    in_index = jnp.arange(out_count + 2 * half_width, dtype=jnp.int32)[None, :]
    offset = in_index - half_width - out_index
    inside = jnp.abs(offset) <= half_width
    offset_real = offset.astype(jnp.float32)
    spread = scales[:, None, None]
    tap_lag = jnp.arange(-half_width, half_width + 1, dtype=jnp.int32).astype(jnp.float32)
    energy = jnp.sum(
        jnp.exp(-(tap_lag[None, :] * tap_lag[None, :]) / (spread[:, :, 0] * spread[:, :, 0])),
        axis=1,
    )
    gaussian = (
        jnp.exp(-(offset_real * offset_real)[None] / (2.0 * spread * spread))
        / jnp.sqrt(energy)[:, None, None]
    )
    return jnp.where(inside[None], gaussian, jnp.zeros_like(gaussian))


def corner_weights(index, frac, count):
    cells = jnp.arange(count, dtype=jnp.int32)[None, :]
    low = jnp.where(cells == index[:, None], (1.0 - frac)[:, None], 0.0)
    high = jnp.where(cells == index[:, None] + 1, frac[:, None], 0.0)
    return low + high


def lat_halo(block, width):
    rows = block.shape[0]
    parts = []
    reach = width
    distance = 1
    below, above = [], []
    while reach > 0:
        take = min(rows, reach)
        below.insert(0, shifted(block[rows - take :], "lat", distance))
        above.append(shifted(block[:take], "lat", -distance))
        reach -= take
        distance += 1
    parts = below + [block] + above
    return jnp.concatenate(parts, axis=0)


def relay_halo_body(count, span, rows, far, x_ref, below_ref, above_ref, relay_ref, send_sem, recv_sem):
    here = lax.axis_index("lat")
    column = lax.axis_index("lon")
    mesh = pl.DeviceIdType.MESH
    half = x_ref.shape[1] // 2
    last = span - 1
    first_of = here % span == 0
    last_of = here % span == last
    up_exists = here + 1 < count
    down_exists = here >= 1
    cross_up = jnp.logical_and(up_exists, (here + 1) % span == 0)
    cross_down = jnp.logical_and(down_exists, first_of)
    low, high = pl.ds(0, half), pl.ds(half, half)
    near_below = below_ref.at[pl.ds(far, rows)]
    near_above = above_ref.at[pl.ds(0, rows)]
    plan = {
        0: (here + 2 < count, 2, x_ref.at[pl.ds(rows - far, far)], below_ref.at[pl.ds(0, far)], here >= 2),
        1: (here >= 2, -2, x_ref.at[pl.ds(0, far)], above_ref.at[pl.ds(rows, far)], here + 2 < count),
        2: (jnp.logical_and(up_exists, jnp.logical_not(cross_up)), 1, x_ref, near_below,
            jnp.logical_and(down_exists, jnp.logical_not(first_of))),
        3: (jnp.logical_and(down_exists, jnp.logical_not(first_of)), -1, x_ref, near_above,
            jnp.logical_and(up_exists, jnp.logical_not(cross_up))),
        4: (cross_up, span, x_ref.at[:, low], relay_ref.at[0], jnp.logical_and(last_of, here >= span)),
        5: (cross_up, 1 - span, x_ref.at[:, high], relay_ref.at[1], jnp.logical_and(first_of, here + span < count)),
        6: (cross_down, -span, x_ref.at[:, low], relay_ref.at[2], jnp.logical_and(first_of, here + span < count)),
        7: (cross_down, span - 1, x_ref.at[:, high], relay_ref.at[3], jnp.logical_and(last_of, here >= span)),
        8: (jnp.logical_and(last_of, here >= span), 1 - span, relay_ref.at[0], near_below.at[:, low],
            jnp.logical_and(first_of, here >= span)),
        9: (jnp.logical_and(first_of, here + span < count), span, relay_ref.at[1], near_below.at[:, high],
            jnp.logical_and(first_of, here >= span)),
        10: (jnp.logical_and(first_of, here + span < count), span - 1, relay_ref.at[2], near_above.at[:, low],
             jnp.logical_and(last_of, up_exists)),
        11: (jnp.logical_and(last_of, here >= span), -span, relay_ref.at[3], near_above.at[:, high],
             jnp.logical_and(last_of, up_exists)),
    }
    feeds = {8: 4, 9: 5, 10: 6, 11: 7}

    barrier = pltpu.get_barrier_semaphore()
    offsets = sorted({offset for _, offset, _, _, _ in plan.values()})
    for offset in offsets:
        neighbour = lax.rem(here + offset + count, count)
        pl.semaphore_signal(barrier, 1, device_id=(neighbour, column), device_id_type=mesh)
    pl.semaphore_wait(barrier, len(offsets))

    def copy(slot, device):
        _, _, src, dst, _ = plan[slot]
        return pltpu.make_async_remote_copy(
            src_ref=src, dst_ref=dst, send_sem=send_sem.at[slot], recv_sem=recv_sem.at[slot],
            device_id=(device, column), device_id_type=mesh,
        )

    def when_start(slot):
        sends, offset, _, _, _ = plan[slot]

        @pl.when(sends)
        def _():
            copy(slot, here + offset).start()

    for slot in range(8):
        when_start(slot)
    for slot, source in feeds.items():
        @pl.when(plan[slot][0])
        def _():
            copy(source, here).wait_recv()
            copy(slot, here + plan[slot][1]).start()
    for slot in range(12):
        sends, offset, _, _, receives = plan[slot]

        @pl.when(sends)
        def _():
            copy(slot, here + offset).wait_send()

        if slot in feeds.values():
            continue

        @pl.when(receives)
        def _():
            copy(slot, here).wait_recv()


def lat_halo_kernel(block, width, span):
    rows = block.shape[0]
    far = width - rows
    count = lax.axis_size("lat")
    halo_shape = jax.ShapeDtypeStruct((width,) + block.shape[1:], block.dtype)
    levels = block.shape[1]
    relay_shape = jax.ShapeDtypeStruct((4, rows, levels // 2, block.shape[2]), block.dtype)
    below, above, _ = pl.pallas_call(
        functools.partial(relay_halo_body, count, span, rows, far),
        out_shape=(halo_shape, halo_shape, relay_shape),
        in_specs=[pl.BlockSpec(memory_space=pl.ANY)],
        out_specs=(pl.BlockSpec(memory_space=pl.ANY),) * 3,
        scratch_shapes=[pltpu.SemaphoreType.DMA((12,)), pltpu.SemaphoreType.DMA((12,))],
        compiler_params=pltpu.CompilerParams(collective_id=0, has_side_effects=True),
    )(block)
    here = lax.axis_index("lat")
    row = jnp.arange(width)[:, None, None]
    below = jnp.where(jnp.where(row >= far, here >= 1, here >= 2), below, 0.0)
    above = jnp.where(jnp.where(row < rows, here + 1 < count, here + 2 < count), above, 0.0)
    return jnp.concatenate([below, block, above], axis=0)


def shards(
    span,
    obs_values, obs_rows, obs_cols, row_frac, col_frac, obs_count, sigma, lat_scales, lon_scales
):
    tile_rows, level_count, tile_cols = sigma.shape
    slot_total = obs_rows.shape[0]
    live_slot = jnp.arange(slot_total, dtype=jnp.int32) < obs_count[0]
    values_t = jnp.where(live_slot[:, None], jnp.transpose(obs_values), 0.0)
    row_w = corner_weights(obs_rows, row_frac, tile_rows + 1)
    col_w = corner_weights(obs_cols, col_frac, tile_cols + 1)
    row_values = row_w[:, :, None] * values_t[:, None, :]
    extended = jnp.einsum(
        "krl,kc->rlc", row_values, col_w, precision=lax.Precision.HIGH
    )
    edge_column = from_behind(extended[:, :, tile_cols], "lon", 1)
    folded = jnp.concatenate(
        [(extended[:, :, 0] + edge_column)[:, :, None], extended[:, :, 1:tile_cols]], axis=2
    )
    edge_row = shifted(folded[tile_rows], "lat", 1)
    departures = jnp.concatenate([(folded[0] + edge_row)[None], folded[1:tile_rows]], axis=0)
    weighted = departures * sigma
    half_width = HALF
    window = lat_halo_kernel(weighted, half_width, span)
    lat_kernel = kernel_matrix(lat_scales, tile_rows, half_width)
    lat_done = jnp.einsum(
        "lip,plc->ilc", lat_kernel, window, precision=lax.Precision.HIGH
    )
    padded_cols = with_halo(lat_done, (("lon", 2),), half_width)
    band = half_width
    lon_kernel = kernel_matrix(lon_scales, band, half_width)
    band_count = tile_cols // band
    bands = jnp.stack(
        [padded_cols[:, :, b * band : b * band + band + 2 * half_width] for b in range(band_count)],
        axis=2,
    )
    result = jnp.einsum("lip,rlbp->rlbi", lon_kernel, bands, precision=lax.Precision.HIGH)
    return result.reshape(tile_rows, level_count, tile_cols)


def lat_groups(mesh):
    column = mesh.devices[:, 0]
    coords = [getattr(device, "coords", None) for device in column]
    if any(c is None for c in coords):
        return tuple(index // 8 for index in range(len(column)))
    return tuple(c[2] // 2 for c in coords)


def solution(mesh):
    in_specs = (
        P(None, ("lat", "lon")),
        P(("lat", "lon")),
        P(("lat", "lon")),
        P(("lat", "lon")),
        P(("lat", "lon")),
        P(("lat", "lon")),
        P("lat", None, "lon"),
        P(),
        P(),
    )
    out_specs = P("lat", None, "lon")
    groups = lat_groups(mesh)
    span = groups.index(groups[0] + 1) if groups[0] + 1 in groups else len(groups)
    return jax.shard_map(functools.partial(shards, span), mesh=mesh, in_specs=in_specs, out_specs=out_specs, check_vma=False)
```

```python
import functools

import jax
import jax.numpy as jnp
from jax import lax
from jax.experimental import pallas as pl
from jax.experimental.pallas import tpu as pltpu
from jax.sharding import PartitionSpec as P

HALF = 128


def from_behind(block, axis, distance):
    devices = range(lax.axis_size(axis))
    route = [((i - distance) % len(devices), i) for i in devices]
    return lax.ppermute(block, axis, route)


def shifted(block, axis, distance):
    devices = range(lax.axis_size(axis))
    route = [(i - distance, i) for i in devices if i - distance in devices]
    return lax.ppermute(block, axis, route)


def with_halo(block, sides, width):
    for axis, dim in sides:
        count = lax.axis_size(axis)
        forward = [(i, i + 1) for i in range(count - 1)]
        forward.append((count - 1, 0))
        backward = [(target, source) for source, target in forward]
        low = lax.ppermute(
            lax.slice_in_dim(block, block.shape[dim] - width, None, axis=dim), axis, forward
        )
        high = lax.ppermute(lax.slice_in_dim(block, 0, width, axis=dim), axis, backward)
        block = jnp.concatenate([low, block, high], axis=dim)
    return block


def kernel_matrix(scales, out_count, half_width):
    out_index = jnp.arange(out_count, dtype=jnp.int32)[:, None]
    in_index = jnp.arange(out_count + 2 * half_width, dtype=jnp.int32)[None, :]
    offset = in_index - half_width - out_index
    inside = jnp.abs(offset) <= half_width
    offset_real = offset.astype(jnp.float32)
    spread = scales[:, None, None]
    tap_lag = jnp.arange(-half_width, half_width + 1, dtype=jnp.int32).astype(jnp.float32)
    energy = jnp.sum(
        jnp.exp(-(tap_lag[None, :] * tap_lag[None, :]) / (spread[:, :, 0] * spread[:, :, 0])),
        axis=1,
    )
    gaussian = (
        jnp.exp(-(offset_real * offset_real)[None] / (2.0 * spread * spread))
        / jnp.sqrt(energy)[:, None, None]
    )
    return jnp.where(inside[None], gaussian, jnp.zeros_like(gaussian))


def corner_weights(index, frac, count):
    cells = jnp.arange(count, dtype=jnp.int32)[None, :]
    low = jnp.where(cells == index[:, None], (1.0 - frac)[:, None], 0.0)
    high = jnp.where(cells == index[:, None] + 1, frac[:, None], 0.0)
    return low + high


def lat_halo(block, width):
    rows = block.shape[0]
    parts = []
    reach = width
    distance = 1
    below, above = [], []
    while reach > 0:
        take = min(rows, reach)
        below.insert(0, shifted(block[rows - take :], "lat", distance))
        above.append(shifted(block[:take], "lat", -distance))
        reach -= take
        distance += 1
    parts = below + [block] + above
    return jnp.concatenate(parts, axis=0)


def relay_halo_body(count, span, rows, far, x_ref, below_ref, above_ref, relay_ref, send_sem, recv_sem):
    here = lax.axis_index("lat")
    column = lax.axis_index("lon")
    mesh = pl.DeviceIdType.MESH
    half = x_ref.shape[1] // 2
    last = span - 1
    first_of = here % span == 0
    last_of = here % span == last
    up_exists = here + 1 < count
    down_exists = here >= 1
    cross_up = jnp.logical_and(up_exists, (here + 1) % span == 0)
    cross_down = jnp.logical_and(down_exists, first_of)
    low, high = pl.ds(0, half), pl.ds(half, half)
    near_below = below_ref.at[pl.ds(far, rows)]
    near_above = above_ref.at[pl.ds(0, rows)]
    plan = {
        0: (here + 2 < count, 2, x_ref.at[pl.ds(rows - far, far)], below_ref.at[pl.ds(0, far)], here >= 2),
        1: (here >= 2, -2, x_ref.at[pl.ds(0, far)], above_ref.at[pl.ds(rows, far)], here + 2 < count),
        2: (jnp.logical_and(up_exists, jnp.logical_not(cross_up)), 1, x_ref, near_below,
            jnp.logical_and(down_exists, jnp.logical_not(first_of))),
        3: (jnp.logical_and(down_exists, jnp.logical_not(first_of)), -1, x_ref, near_above,
            jnp.logical_and(up_exists, jnp.logical_not(cross_up))),
        4: (cross_up, span, x_ref.at[:, low], relay_ref.at[0], jnp.logical_and(last_of, here >= span)),
        5: (cross_up, 1 - span, x_ref.at[:, high], relay_ref.at[1], jnp.logical_and(first_of, here + span < count)),
        6: (cross_down, -span, x_ref.at[:, low], relay_ref.at[2], jnp.logical_and(first_of, here + span < count)),
        7: (cross_down, span - 1, x_ref.at[:, high], relay_ref.at[3], jnp.logical_and(last_of, here >= span)),
        8: (jnp.logical_and(last_of, here >= span), 1 - span, relay_ref.at[0], near_below.at[:, low],
            jnp.logical_and(first_of, here >= span)),
        9: (jnp.logical_and(first_of, here + span < count), span, relay_ref.at[1], near_below.at[:, high],
            jnp.logical_and(first_of, here >= span)),
        10: (jnp.logical_and(first_of, here + span < count), span - 1, relay_ref.at[2], near_above.at[:, low],
             jnp.logical_and(last_of, up_exists)),
        11: (jnp.logical_and(last_of, here >= span), -span, relay_ref.at[3], near_above.at[:, high],
             jnp.logical_and(last_of, up_exists)),
    }
    feeds = {8: 4, 9: 5, 10: 6, 11: 7}

    barrier = pltpu.get_barrier_semaphore()
    offsets = sorted({offset for _, offset, _, _, _ in plan.values()})
    for offset in offsets:
        neighbour = lax.rem(here + offset + count, count)
        pl.semaphore_signal(barrier, 1, device_id=(neighbour, column), device_id_type=mesh)
    pl.semaphore_wait(barrier, len(offsets))

    def copy(slot, device):
        _, _, src, dst, _ = plan[slot]
        return pltpu.make_async_remote_copy(
            src_ref=src, dst_ref=dst, send_sem=send_sem.at[slot], recv_sem=recv_sem.at[slot],
            device_id=(device, column), device_id_type=mesh,
        )

    def when_start(slot):
        sends, offset, _, _, _ = plan[slot]

        @pl.when(sends)
        def _():
            copy(slot, here + offset).start()

    for slot in range(8):
        when_start(slot)
    for slot, source in feeds.items():
        @pl.when(plan[slot][0])
        def _():
            copy(source, here).wait_recv()
            copy(slot, here + plan[slot][1]).start()
    for slot in range(12):
        sends, offset, _, _, receives = plan[slot]

        @pl.when(sends)
        def _():
            copy(slot, here + offset).wait_send()

        if slot in feeds.values():
            continue

        @pl.when(receives)
        def _():
            copy(slot, here).wait_recv()


def lat_halo_kernel(block, width, span):
    rows = block.shape[0]
    far = width - rows
    count = lax.axis_size("lat")
    halo_shape = jax.ShapeDtypeStruct((width,) + block.shape[1:], block.dtype)
    levels = block.shape[1]
    relay_shape = jax.ShapeDtypeStruct((4, rows, levels // 2, block.shape[2]), block.dtype)
    below, above, _ = pl.pallas_call(
        functools.partial(relay_halo_body, count, span, rows, far),
        out_shape=(halo_shape, halo_shape, relay_shape),
        in_specs=[pl.BlockSpec(memory_space=pl.ANY)],
        out_specs=(pl.BlockSpec(memory_space=pl.ANY),) * 3,
        scratch_shapes=[pltpu.SemaphoreType.DMA((12,)), pltpu.SemaphoreType.DMA((12,))],
        compiler_params=pltpu.CompilerParams(collective_id=0, has_side_effects=True),
    )(block)
    here = lax.axis_index("lat")
    row = jnp.arange(width)[:, None, None]
    below = jnp.where(jnp.where(row >= far, here >= 1, here >= 2), below, 0.0)
    above = jnp.where(jnp.where(row < rows, here + 1 < count, here + 2 < count), above, 0.0)
    return jnp.concatenate([below, block, above], axis=0)


def lon_halo_body(count, width, x_ref, west_ref, east_ref, send_sem, recv_sem):
    here = lax.axis_index("lon")
    row = lax.axis_index("lat")
    mesh = pl.DeviceIdType.MESH
    cols = x_ref.shape[2]
    east = lax.rem(here + 1, count)
    west = lax.rem(here + count - 1, count)
    barrier = pltpu.get_barrier_semaphore()
    for neighbour in (west, east):
        pl.semaphore_signal(barrier, 1, device_id=(row, neighbour), device_id_type=mesh)
    pl.semaphore_wait(barrier, 2)
    copies = [
        pltpu.make_async_remote_copy(
            src_ref=x_ref.at[:, :, pl.ds(cols - width, width)], dst_ref=west_ref,
            send_sem=send_sem.at[0], recv_sem=recv_sem.at[0],
            device_id=(row, east), device_id_type=mesh,
        ),
        pltpu.make_async_remote_copy(
            src_ref=x_ref.at[:, :, pl.ds(0, width)], dst_ref=east_ref,
            send_sem=send_sem.at[1], recv_sem=recv_sem.at[1],
            device_id=(row, west), device_id_type=mesh,
        ),
    ]
    for copy in copies:
        copy.start()
    for copy in copies:
        copy.wait()


def lon_halo_kernel(block, width):
    count = lax.axis_size("lon")
    edge = jax.ShapeDtypeStruct(block.shape[:2] + (width,), block.dtype)
    west, east = pl.pallas_call(
        functools.partial(lon_halo_body, count, width),
        out_shape=(edge, edge),
        in_specs=[pl.BlockSpec(memory_space=pl.ANY)],
        out_specs=(pl.BlockSpec(memory_space=pl.ANY),) * 2,
        scratch_shapes=[pltpu.SemaphoreType.DMA((2,)), pltpu.SemaphoreType.DMA((2,))],
        compiler_params=pltpu.CompilerParams(collective_id=1, has_side_effects=True),
    )(block)
    return jnp.concatenate([west, block, east], axis=2)


def shards(
    span,
    obs_values, obs_rows, obs_cols, row_frac, col_frac, obs_count, sigma, lat_scales, lon_scales
):
    tile_rows, level_count, tile_cols = sigma.shape
    slot_total = obs_rows.shape[0]
    live_slot = jnp.arange(slot_total, dtype=jnp.int32) < obs_count[0]
    values_t = jnp.where(live_slot[:, None], jnp.transpose(obs_values), 0.0)
    row_w = corner_weights(obs_rows, row_frac, tile_rows + 1)
    col_w = corner_weights(obs_cols, col_frac, tile_cols + 1)
    row_values = row_w[:, :, None] * values_t[:, None, :]
    extended = jnp.einsum(
        "krl,kc->rlc", row_values, col_w, precision=lax.Precision.HIGH
    )
    edge_column = from_behind(extended[:, :, tile_cols], "lon", 1)
    folded = jnp.concatenate(
        [(extended[:, :, 0] + edge_column)[:, :, None], extended[:, :, 1:tile_cols]], axis=2
    )
    edge_row = shifted(folded[tile_rows], "lat", 1)
    departures = jnp.concatenate([(folded[0] + edge_row)[None], folded[1:tile_rows]], axis=0)
    weighted = departures * sigma
    half_width = HALF
    window = lat_halo_kernel(weighted, half_width, span)
    lat_kernel = kernel_matrix(lat_scales, tile_rows, half_width)
    lat_done = jnp.einsum(
        "lip,plc->ilc", lat_kernel, window, precision=lax.Precision.HIGH
    )
    padded_cols = lon_halo_kernel(lat_done, half_width)
    band = half_width
    lon_kernel = kernel_matrix(lon_scales, band, half_width)
    band_count = tile_cols // band
    bands = jnp.stack(
        [padded_cols[:, :, b * band : b * band + band + 2 * half_width] for b in range(band_count)],
        axis=2,
    )
    result = jnp.einsum("lip,rlbp->rlbi", lon_kernel, bands, precision=lax.Precision.HIGH)
    return result.reshape(tile_rows, level_count, tile_cols)


def lat_groups(mesh):
    column = mesh.devices[:, 0]
    coords = [getattr(device, "coords", None) for device in column]
    if any(c is None for c in coords):
        return tuple(index // 8 for index in range(len(column)))
    return tuple(c[2] // 2 for c in coords)


def solution(mesh):
    in_specs = (
        P(None, ("lat", "lon")),
        P(("lat", "lon")),
        P(("lat", "lon")),
        P(("lat", "lon")),
        P(("lat", "lon")),
        P(("lat", "lon")),
        P("lat", None, "lon"),
        P(),
        P(),
    )
    out_specs = P("lat", None, "lon")
    groups = lat_groups(mesh)
    span = groups.index(groups[0] + 1) if groups[0] + 1 in groups else len(groups)
    return jax.shard_map(functools.partial(shards, span), mesh=mesh, in_specs=in_specs, out_specs=out_specs, check_vma=False)
```

```python
import functools

import jax
import jax.numpy as jnp
from jax import lax
from jax.experimental import pallas as pl
from jax.experimental.pallas import tpu as pltpu
from jax.sharding import PartitionSpec as P

HALF = 128


def from_behind(block, axis, distance):
    devices = range(lax.axis_size(axis))
    route = [((i - distance) % len(devices), i) for i in devices]
    return lax.ppermute(block, axis, route)


def shifted(block, axis, distance):
    devices = range(lax.axis_size(axis))
    route = [(i - distance, i) for i in devices if i - distance in devices]
    return lax.ppermute(block, axis, route)


def with_halo(block, sides, width):
    for axis, dim in sides:
        count = lax.axis_size(axis)
        forward = [(i, i + 1) for i in range(count - 1)]
        forward.append((count - 1, 0))
        backward = [(target, source) for source, target in forward]
        low = lax.ppermute(
            lax.slice_in_dim(block, block.shape[dim] - width, None, axis=dim), axis, forward
        )
        high = lax.ppermute(lax.slice_in_dim(block, 0, width, axis=dim), axis, backward)
        block = jnp.concatenate([low, block, high], axis=dim)
    return block


def kernel_matrix(scales, out_count, half_width):
    out_index = jnp.arange(out_count, dtype=jnp.int32)[:, None]
    in_index = jnp.arange(out_count + 2 * half_width, dtype=jnp.int32)[None, :]
    offset = in_index - half_width - out_index
    inside = jnp.abs(offset) <= half_width
    offset_real = offset.astype(jnp.float32)
    spread = scales[:, None, None]
    tap_lag = jnp.arange(-half_width, half_width + 1, dtype=jnp.int32).astype(jnp.float32)
    energy = jnp.sum(
        jnp.exp(-(tap_lag[None, :] * tap_lag[None, :]) / (spread[:, :, 0] * spread[:, :, 0])),
        axis=1,
    )
    gaussian = (
        jnp.exp(-(offset_real * offset_real)[None] / (2.0 * spread * spread))
        / jnp.sqrt(energy)[:, None, None]
    )
    return jnp.where(inside[None], gaussian, jnp.zeros_like(gaussian))


def corner_weights(index, frac, count):
    cells = jnp.arange(count, dtype=jnp.int32)[None, :]
    low = jnp.where(cells == index[:, None], (1.0 - frac)[:, None], 0.0)
    high = jnp.where(cells == index[:, None] + 1, frac[:, None], 0.0)
    return low + high


def lat_halo(block, width):
    rows = block.shape[0]
    parts = []
    reach = width
    distance = 1
    below, above = [], []
    while reach > 0:
        take = min(rows, reach)
        below.insert(0, shifted(block[rows - take :], "lat", distance))
        above.append(shifted(block[:take], "lat", -distance))
        reach -= take
        distance += 1
    parts = below + [block] + above
    return jnp.concatenate(parts, axis=0)


def relay_halo_body(count, span, rows, far, x_ref, below_ref, above_ref, relay_ref, send_sem, recv_sem):
    here = lax.axis_index("lat")
    column = lax.axis_index("lon")
    mesh = pl.DeviceIdType.MESH
    half = x_ref.shape[1] // 2
    last = span - 1
    first_of = here % span == 0
    last_of = here % span == last
    up_exists = here + 1 < count
    down_exists = here >= 1
    cross_up = jnp.logical_and(up_exists, (here + 1) % span == 0)
    cross_down = jnp.logical_and(down_exists, first_of)
    low, high = pl.ds(0, half), pl.ds(half, half)
    near_below = below_ref.at[pl.ds(far, rows)]
    near_above = above_ref.at[pl.ds(0, rows)]
    plan = {
        0: (here + 2 < count, 2, x_ref.at[pl.ds(rows - far, far)], below_ref.at[pl.ds(0, far)], here >= 2),
        1: (here >= 2, -2, x_ref.at[pl.ds(0, far)], above_ref.at[pl.ds(rows, far)], here + 2 < count),
        2: (jnp.logical_and(up_exists, jnp.logical_not(cross_up)), 1, x_ref, near_below,
            jnp.logical_and(down_exists, jnp.logical_not(first_of))),
        3: (jnp.logical_and(down_exists, jnp.logical_not(first_of)), -1, x_ref, near_above,
            jnp.logical_and(up_exists, jnp.logical_not(cross_up))),
        4: (cross_up, span, x_ref.at[:, low], relay_ref.at[0], jnp.logical_and(last_of, here >= span)),
        5: (cross_up, 1 - span, x_ref.at[:, high], relay_ref.at[1], jnp.logical_and(first_of, here + span < count)),
        6: (cross_down, -span, x_ref.at[:, low], relay_ref.at[2], jnp.logical_and(first_of, here + span < count)),
        7: (cross_down, span - 1, x_ref.at[:, high], relay_ref.at[3], jnp.logical_and(last_of, here >= span)),
        8: (jnp.logical_and(last_of, here >= span), 1 - span, relay_ref.at[0], near_below.at[:, low],
            jnp.logical_and(first_of, here >= span)),
        9: (jnp.logical_and(first_of, here + span < count), span, relay_ref.at[1], near_below.at[:, high],
            jnp.logical_and(first_of, here >= span)),
        10: (jnp.logical_and(first_of, here + span < count), span - 1, relay_ref.at[2], near_above.at[:, low],
             jnp.logical_and(last_of, up_exists)),
        11: (jnp.logical_and(last_of, here >= span), -span, relay_ref.at[3], near_above.at[:, high],
             jnp.logical_and(last_of, up_exists)),
    }
    feeds = {8: 4, 9: 5, 10: 6, 11: 7}

    barrier = pltpu.get_barrier_semaphore()
    offsets = sorted({offset for _, offset, _, _, _ in plan.values()})
    for offset in offsets:
        neighbour = lax.rem(here + offset + count, count)
        pl.semaphore_signal(barrier, 1, device_id=(neighbour, column), device_id_type=mesh)
    pl.semaphore_wait(barrier, len(offsets))

    def copy(slot, device):
        _, _, src, dst, _ = plan[slot]
        return pltpu.make_async_remote_copy(
            src_ref=src, dst_ref=dst, send_sem=send_sem.at[slot], recv_sem=recv_sem.at[slot],
            device_id=(device, column), device_id_type=mesh,
        )

    def when_start(slot):
        sends, offset, _, _, _ = plan[slot]

        @pl.when(sends)
        def _():
            copy(slot, here + offset).start()

    for slot in range(8):
        when_start(slot)
    for slot, source in feeds.items():
        @pl.when(plan[slot][0])
        def _():
            copy(source, here).wait_recv()
            copy(slot, here + plan[slot][1]).start()
    for slot in range(12):
        sends, offset, _, _, receives = plan[slot]

        @pl.when(sends)
        def _():
            copy(slot, here + offset).wait_send()

        if slot in feeds.values():
            continue

        @pl.when(receives)
        def _():
            copy(slot, here).wait_recv()


def lat_halo_kernel(block, width, span):
    rows = block.shape[0]
    far = width - rows
    count = lax.axis_size("lat")
    halo_shape = jax.ShapeDtypeStruct((width,) + block.shape[1:], block.dtype)
    levels = block.shape[1]
    relay_shape = jax.ShapeDtypeStruct((4, rows, levels // 2, block.shape[2]), block.dtype)
    below, above, _ = pl.pallas_call(
        functools.partial(relay_halo_body, count, span, rows, far),
        out_shape=(halo_shape, halo_shape, relay_shape),
        in_specs=[pl.BlockSpec(memory_space=pl.ANY)],
        out_specs=(pl.BlockSpec(memory_space=pl.ANY),) * 3,
        scratch_shapes=[pltpu.SemaphoreType.DMA((12,)), pltpu.SemaphoreType.DMA((12,))],
        compiler_params=pltpu.CompilerParams(collective_id=0, has_side_effects=True),
    )(block)
    here = lax.axis_index("lat")
    row = jnp.arange(width)[:, None, None]
    below = jnp.where(jnp.where(row >= far, here >= 1, here >= 2), below, 0.0)
    above = jnp.where(jnp.where(row < rows, here + 1 < count, here + 2 < count), above, 0.0)
    return jnp.concatenate([below, block, above], axis=0)


def lon_halo_body(count, width, x_ref, west_ref, east_ref, send_sem, recv_sem):
    here = lax.axis_index("lon")
    row = lax.axis_index("lat")
    mesh = pl.DeviceIdType.MESH
    cols = x_ref.shape[0]
    east = lax.rem(here + 1, count)
    west = lax.rem(here + count - 1, count)
    barrier = pltpu.get_barrier_semaphore()
    for neighbour in (west, east):
        pl.semaphore_signal(barrier, 1, device_id=(row, neighbour), device_id_type=mesh)
    pl.semaphore_wait(barrier, 2)
    copies = [
        pltpu.make_async_remote_copy(
            src_ref=x_ref.at[pl.ds(cols - width, width)], dst_ref=west_ref,
            send_sem=send_sem.at[0], recv_sem=recv_sem.at[0],
            device_id=(row, east), device_id_type=mesh,
        ),
        pltpu.make_async_remote_copy(
            src_ref=x_ref.at[pl.ds(0, width)], dst_ref=east_ref,
            send_sem=send_sem.at[1], recv_sem=recv_sem.at[1],
            device_id=(row, west), device_id_type=mesh,
        ),
    ]
    for copy in copies:
        copy.start()
    for copy in copies:
        copy.wait()


def lon_halo_kernel(block, width):
    count = lax.axis_size("lon")
    edge = jax.ShapeDtypeStruct((width,) + block.shape[1:], block.dtype)
    west, east = pl.pallas_call(
        functools.partial(lon_halo_body, count, width),
        out_shape=(edge, edge),
        in_specs=[pl.BlockSpec(memory_space=pl.ANY)],
        out_specs=(pl.BlockSpec(memory_space=pl.ANY),) * 2,
        scratch_shapes=[pltpu.SemaphoreType.DMA((2,)), pltpu.SemaphoreType.DMA((2,))],
        compiler_params=pltpu.CompilerParams(collective_id=1, has_side_effects=True),
    )(block)
    return jnp.concatenate([west, block, east], axis=0)


def shards(
    span,
    obs_values, obs_rows, obs_cols, row_frac, col_frac, obs_count, sigma, lat_scales, lon_scales
):
    tile_rows, level_count, tile_cols = sigma.shape
    slot_total = obs_rows.shape[0]
    live_slot = jnp.arange(slot_total, dtype=jnp.int32) < obs_count[0]
    values_t = jnp.where(live_slot[:, None], jnp.transpose(obs_values), 0.0)
    row_w = corner_weights(obs_rows, row_frac, tile_rows + 1)
    col_w = corner_weights(obs_cols, col_frac, tile_cols + 1)
    row_values = row_w[:, :, None] * values_t[:, None, :]
    extended = jnp.einsum(
        "krl,kc->rlc", row_values, col_w, precision=lax.Precision.HIGH
    )
    edge_column = from_behind(extended[:, :, tile_cols], "lon", 1)
    folded = jnp.concatenate(
        [(extended[:, :, 0] + edge_column)[:, :, None], extended[:, :, 1:tile_cols]], axis=2
    )
    edge_row = shifted(folded[tile_rows], "lat", 1)
    departures = jnp.concatenate([(folded[0] + edge_row)[None], folded[1:tile_rows]], axis=0)
    weighted = departures * sigma
    half_width = HALF
    window = lat_halo_kernel(weighted, half_width, span)
    lat_kernel = kernel_matrix(lat_scales, tile_rows, half_width)
    lat_done = jnp.einsum(
        "lip,plc->cli", lat_kernel, window, precision=lax.Precision.HIGH
    )
    padded_cols = lon_halo_kernel(lat_done, half_width)
    band = half_width
    lon_kernel = kernel_matrix(lon_scales, band, half_width)
    band_count = tile_cols // band
    bands = jnp.stack(
        [padded_cols[b * band : b * band + band + 2 * half_width] for b in range(band_count)],
        axis=0,
    )
    result = jnp.einsum("lip,bplr->rlbi", lon_kernel, bands, precision=lax.Precision.HIGH)
    return result.reshape(tile_rows, level_count, tile_cols)


def lat_groups(mesh):
    column = mesh.devices[:, 0]
    coords = [getattr(device, "coords", None) for device in column]
    if any(c is None for c in coords):
        return tuple(index // 8 for index in range(len(column)))
    return tuple(c[2] // 2 for c in coords)


def solution(mesh):
    in_specs = (
        P(None, ("lat", "lon")),
        P(("lat", "lon")),
        P(("lat", "lon")),
        P(("lat", "lon")),
        P(("lat", "lon")),
        P(("lat", "lon")),
        P("lat", None, "lon"),
        P(),
        P(),
    )
    out_specs = P("lat", None, "lon")
    groups = lat_groups(mesh)
    span = groups.index(groups[0] + 1) if groups[0] + 1 in groups else len(groups)
    return jax.shard_map(functools.partial(shards, span), mesh=mesh, in_specs=in_specs, out_specs=out_specs, check_vma=False)
```

```python
import functools

import jax
import jax.numpy as jnp
from jax import lax
from jax.experimental import pallas as pl
from jax.experimental.pallas import tpu as pltpu
from jax.sharding import PartitionSpec as P

HALF = 128


def from_behind(block, axis, distance):
    devices = range(lax.axis_size(axis))
    route = [((i - distance) % len(devices), i) for i in devices]
    return lax.ppermute(block, axis, route)


def shifted(block, axis, distance):
    devices = range(lax.axis_size(axis))
    route = [(i - distance, i) for i in devices if i - distance in devices]
    return lax.ppermute(block, axis, route)


def with_halo(block, sides, width):
    for axis, dim in sides:
        count = lax.axis_size(axis)
        forward = [(i, i + 1) for i in range(count - 1)]
        forward.append((count - 1, 0))
        backward = [(target, source) for source, target in forward]
        low = lax.ppermute(
            lax.slice_in_dim(block, block.shape[dim] - width, None, axis=dim), axis, forward
        )
        high = lax.ppermute(lax.slice_in_dim(block, 0, width, axis=dim), axis, backward)
        block = jnp.concatenate([low, block, high], axis=dim)
    return block


def kernel_matrix(scales, out_count, half_width):
    out_index = jnp.arange(out_count, dtype=jnp.int32)[:, None]
    in_index = jnp.arange(out_count + 2 * half_width, dtype=jnp.int32)[None, :]
    offset = in_index - half_width - out_index
    inside = jnp.abs(offset) <= half_width
    offset_real = offset.astype(jnp.float32)
    spread = scales[:, None, None]
    tap_lag = jnp.arange(-half_width, half_width + 1, dtype=jnp.int32).astype(jnp.float32)
    energy = jnp.sum(
        jnp.exp(-(tap_lag[None, :] * tap_lag[None, :]) / (spread[:, :, 0] * spread[:, :, 0])),
        axis=1,
    )
    gaussian = (
        jnp.exp(-(offset_real * offset_real)[None] / (2.0 * spread * spread))
        / jnp.sqrt(energy)[:, None, None]
    )
    return jnp.where(inside[None], gaussian, jnp.zeros_like(gaussian))


def corner_weights(index, frac, count):
    cells = jnp.arange(count, dtype=jnp.int32)[None, :]
    low = jnp.where(cells == index[:, None], (1.0 - frac)[:, None], 0.0)
    high = jnp.where(cells == index[:, None] + 1, frac[:, None], 0.0)
    return low + high


def lat_halo(block, width):
    rows = block.shape[0]
    parts = []
    reach = width
    distance = 1
    below, above = [], []
    while reach > 0:
        take = min(rows, reach)
        below.insert(0, shifted(block[rows - take :], "lat", distance))
        above.append(shifted(block[:take], "lat", -distance))
        reach -= take
        distance += 1
    parts = below + [block] + above
    return jnp.concatenate(parts, axis=0)


def relay_halo_body(count, span, rows, far, x_ref, below_ref, above_ref, relay_ref, send_sem, recv_sem):
    here = lax.axis_index("lat")
    column = lax.axis_index("lon")
    mesh = pl.DeviceIdType.MESH
    half = x_ref.shape[1] // 2
    last = span - 1
    first_of = here % span == 0
    last_of = here % span == last
    up_exists = here + 1 < count
    down_exists = here >= 1
    cross_up = jnp.logical_and(up_exists, (here + 1) % span == 0)
    cross_down = jnp.logical_and(down_exists, first_of)
    low, high = pl.ds(0, half), pl.ds(half, half)
    near_below = below_ref.at[pl.ds(far, rows)]
    near_above = above_ref.at[pl.ds(0, rows)]
    plan = {
        0: (here + 2 < count, 2, x_ref.at[pl.ds(rows - far, far)], below_ref.at[pl.ds(0, far)], here >= 2),
        1: (here >= 2, -2, x_ref.at[pl.ds(0, far)], above_ref.at[pl.ds(rows, far)], here + 2 < count),
        2: (jnp.logical_and(up_exists, jnp.logical_not(cross_up)), 1, x_ref, near_below,
            jnp.logical_and(down_exists, jnp.logical_not(first_of))),
        3: (jnp.logical_and(down_exists, jnp.logical_not(first_of)), -1, x_ref, near_above,
            jnp.logical_and(up_exists, jnp.logical_not(cross_up))),
        4: (cross_up, span, x_ref.at[:, low], relay_ref.at[0], jnp.logical_and(last_of, here >= span)),
        5: (cross_up, 1 - span, x_ref.at[:, high], relay_ref.at[1], jnp.logical_and(first_of, here + span < count)),
        6: (cross_down, -span, x_ref.at[:, low], relay_ref.at[2], jnp.logical_and(first_of, here + span < count)),
        7: (cross_down, span - 1, x_ref.at[:, high], relay_ref.at[3], jnp.logical_and(last_of, here >= span)),
        8: (jnp.logical_and(last_of, here >= span), 1 - span, relay_ref.at[0], near_below.at[:, low],
            jnp.logical_and(first_of, here >= span)),
        9: (jnp.logical_and(first_of, here + span < count), span, relay_ref.at[1], near_below.at[:, high],
            jnp.logical_and(first_of, here >= span)),
        10: (jnp.logical_and(first_of, here + span < count), span - 1, relay_ref.at[2], near_above.at[:, low],
             jnp.logical_and(last_of, up_exists)),
        11: (jnp.logical_and(last_of, here >= span), -span, relay_ref.at[3], near_above.at[:, high],
             jnp.logical_and(last_of, up_exists)),
    }
    feeds = {8: 4, 9: 5, 10: 6, 11: 7}

    barrier = pltpu.get_barrier_semaphore()
    offsets = sorted({offset for _, offset, _, _, _ in plan.values()})
    for offset in offsets:
        neighbour = lax.rem(here + offset + count, count)
        pl.semaphore_signal(barrier, 1, device_id=(neighbour, column), device_id_type=mesh)
    pl.semaphore_wait(barrier, len(offsets))

    def copy(slot, device):
        _, _, src, dst, _ = plan[slot]
        return pltpu.make_async_remote_copy(
            src_ref=src, dst_ref=dst, send_sem=send_sem.at[slot], recv_sem=recv_sem.at[slot],
            device_id=(device, column), device_id_type=mesh,
        )

    def when_start(slot):
        sends, offset, _, _, _ = plan[slot]

        @pl.when(sends)
        def _():
            copy(slot, here + offset).start()

    for slot in range(8):
        when_start(slot)
    for slot, source in feeds.items():
        @pl.when(plan[slot][0])
        def _():
            copy(source, here).wait_recv()
            copy(slot, here + plan[slot][1]).start()
    for slot in range(12):
        sends, offset, _, _, receives = plan[slot]

        @pl.when(sends)
        def _():
            copy(slot, here + offset).wait_send()

        if slot in feeds.values():
            continue

        @pl.when(receives)
        def _():
            copy(slot, here).wait_recv()


def lat_halo_kernel(block, width, span):
    rows = block.shape[0]
    far = width - rows
    count = lax.axis_size("lat")
    halo_shape = jax.ShapeDtypeStruct((width,) + block.shape[1:], block.dtype)
    levels = block.shape[1]
    relay_shape = jax.ShapeDtypeStruct((4, rows, levels // 2, block.shape[2]), block.dtype)
    below, above, _ = pl.pallas_call(
        functools.partial(relay_halo_body, count, span, rows, far),
        out_shape=(halo_shape, halo_shape, relay_shape),
        in_specs=[pl.BlockSpec(memory_space=pl.ANY)],
        out_specs=(pl.BlockSpec(memory_space=pl.ANY),) * 3,
        scratch_shapes=[pltpu.SemaphoreType.DMA((12,)), pltpu.SemaphoreType.DMA((12,))],
        compiler_params=pltpu.CompilerParams(collective_id=0, has_side_effects=True),
    )(block)
    here = lax.axis_index("lat")
    row = jnp.arange(width)[:, None, None]
    below = jnp.where(jnp.where(row >= far, here >= 1, here >= 2), below, 0.0)
    above = jnp.where(jnp.where(row < rows, here + 1 < count, here + 2 < count), above, 0.0)
    return jnp.concatenate([below, block, above], axis=0)


def shards(
    span,
    obs_values, obs_rows, obs_cols, row_frac, col_frac, obs_count, sigma, lat_scales, lon_scales
):
    tile_rows, level_count, tile_cols = sigma.shape
    slot_total = obs_rows.shape[0]
    live_slot = jnp.arange(slot_total, dtype=jnp.int32) < obs_count[0]
    values_t = jnp.where(live_slot[:, None], jnp.transpose(obs_values), 0.0)
    row_w = corner_weights(obs_rows, row_frac, tile_rows + 1)
    col_w = corner_weights(obs_cols, col_frac, tile_cols + 1)
    row_values = values_t[:, :, None] * row_w[:, None, :]
    extended = jnp.einsum(
        "klr,kc->rlc", row_values, col_w, precision=lax.Precision.HIGH
    )
    edge_column = from_behind(extended[:, :, tile_cols], "lon", 1)
    folded = jnp.concatenate(
        [(extended[:, :, 0] + edge_column)[:, :, None], extended[:, :, 1:tile_cols]], axis=2
    )
    edge_row = shifted(folded[tile_rows], "lat", 1)
    departures = jnp.concatenate([(folded[0] + edge_row)[None], folded[1:tile_rows]], axis=0)
    weighted = departures * sigma
    half_width = HALF
    window = lat_halo_kernel(weighted, half_width, span)
    lat_kernel = kernel_matrix(lat_scales, tile_rows, half_width)
    lat_done = jnp.einsum(
        "lip,plc->ilc", lat_kernel, window, precision=lax.Precision.HIGH
    )
    padded_cols = with_halo(lat_done, (("lon", 2),), half_width)
    band = half_width
    lon_kernel = kernel_matrix(lon_scales, band, half_width)
    band_count = tile_cols // band
    bands = jnp.stack(
        [padded_cols[:, :, b * band : b * band + band + 2 * half_width] for b in range(band_count)],
        axis=2,
    )
    result = jnp.einsum("lip,rlbp->rlbi", lon_kernel, bands, precision=lax.Precision.HIGH)
    return result.reshape(tile_rows, level_count, tile_cols)


def lat_groups(mesh):
    column = mesh.devices[:, 0]
    coords = [getattr(device, "coords", None) for device in column]
    if any(c is None for c in coords):
        return tuple(index // 8 for index in range(len(column)))
    return tuple(c[2] // 2 for c in coords)


def solution(mesh):
    in_specs = (
        P(None, ("lat", "lon")),
        P(("lat", "lon")),
        P(("lat", "lon")),
        P(("lat", "lon")),
        P(("lat", "lon")),
        P(("lat", "lon")),
        P("lat", None, "lon"),
        P(),
        P(),
    )
    out_specs = P("lat", None, "lon")
    groups = lat_groups(mesh)
    span = groups.index(groups[0] + 1) if groups[0] + 1 in groups else len(groups)
    return jax.shard_map(functools.partial(shards, span), mesh=mesh, in_specs=in_specs, out_specs=out_specs, check_vma=False)
```

```python
import functools

import jax
import jax.numpy as jnp
from jax import lax
from jax.experimental import pallas as pl
from jax.experimental.pallas import tpu as pltpu
from jax.sharding import PartitionSpec as P

HALF = 128


def from_behind(block, axis, distance):
    devices = range(lax.axis_size(axis))
    route = [((i - distance) % len(devices), i) for i in devices]
    return lax.ppermute(block, axis, route)


def shifted(block, axis, distance):
    devices = range(lax.axis_size(axis))
    route = [(i - distance, i) for i in devices if i - distance in devices]
    return lax.ppermute(block, axis, route)


def with_halo(block, sides, width):
    for axis, dim in sides:
        count = lax.axis_size(axis)
        forward = [(i, i + 1) for i in range(count - 1)]
        forward.append((count - 1, 0))
        backward = [(target, source) for source, target in forward]
        low = lax.ppermute(
            lax.slice_in_dim(block, block.shape[dim] - width, None, axis=dim), axis, forward
        )
        high = lax.ppermute(lax.slice_in_dim(block, 0, width, axis=dim), axis, backward)
        block = jnp.concatenate([low, block, high], axis=dim)
    return block


def kernel_matrix(scales, out_count, half_width):
    out_index = jnp.arange(out_count, dtype=jnp.int32)[:, None]
    in_index = jnp.arange(out_count + 2 * half_width, dtype=jnp.int32)[None, :]
    offset = in_index - half_width - out_index
    inside = jnp.abs(offset) <= half_width
    offset_real = offset.astype(jnp.float32)
    spread = scales[:, None, None]
    tap_lag = jnp.arange(-half_width, half_width + 1, dtype=jnp.int32).astype(jnp.float32)
    energy = jnp.sum(
        jnp.exp(-(tap_lag[None, :] * tap_lag[None, :]) / (spread[:, :, 0] * spread[:, :, 0])),
        axis=1,
    )
    gaussian = (
        jnp.exp(-(offset_real * offset_real)[None] / (2.0 * spread * spread))
        / jnp.sqrt(energy)[:, None, None]
    )
    return jnp.where(inside[None], gaussian, jnp.zeros_like(gaussian))


def corner_weights(index, frac, count):
    cells = jnp.arange(count, dtype=jnp.int32)[None, :]
    low = jnp.where(cells == index[:, None], (1.0 - frac)[:, None], 0.0)
    high = jnp.where(cells == index[:, None] + 1, frac[:, None], 0.0)
    return low + high


def lat_halo(block, width):
    rows = block.shape[0]
    parts = []
    reach = width
    distance = 1
    below, above = [], []
    while reach > 0:
        take = min(rows, reach)
        below.insert(0, shifted(block[rows - take :], "lat", distance))
        above.append(shifted(block[:take], "lat", -distance))
        reach -= take
        distance += 1
    parts = below + [block] + above
    return jnp.concatenate(parts, axis=0)


def relay_halo_body(count, span, pieces, rows, far, x_ref, below_ref, above_ref, relay_ref, send_sem, recv_sem):
    here = lax.axis_index("lat")
    column = lax.axis_index("lon")
    mesh = pl.DeviceIdType.MESH
    half = x_ref.shape[1] // 2
    last = span - 1
    first_of = here % span == 0
    last_of = here % span == last
    up_exists = here + 1 < count
    down_exists = here >= 1
    cross_up = jnp.logical_and(up_exists, (here + 1) % span == 0)
    cross_down = jnp.logical_and(down_exists, first_of)
    low, high = pl.ds(0, half), pl.ds(half, half)
    near_below = below_ref.at[pl.ds(far, rows)]
    near_above = above_ref.at[pl.ds(0, rows)]
    plan = [
        (here + 2 < count, 2, x_ref.at[pl.ds(rows - far, far)], below_ref.at[pl.ds(0, far)], here >= 2),
        (here >= 2, -2, x_ref.at[pl.ds(0, far)], above_ref.at[pl.ds(rows, far)], here + 2 < count),
        (jnp.logical_and(up_exists, jnp.logical_not(cross_up)), 1, x_ref, near_below,
         jnp.logical_and(down_exists, jnp.logical_not(first_of))),
        (jnp.logical_and(down_exists, jnp.logical_not(first_of)), -1, x_ref, near_above,
         jnp.logical_and(up_exists, jnp.logical_not(cross_up))),
    ]
    feeds = {}
    relay_up_a = jnp.logical_and(last_of, here >= span)
    relay_up_b = jnp.logical_and(first_of, here + span < count)
    lands_below = jnp.logical_and(first_of, here >= span)
    lands_above = jnp.logical_and(last_of, up_exists)
    routes = [
        (cross_up, span, low, 0, relay_up_a, 1 - span, near_below, lands_below),
        (cross_up, 1 - span, high, 1, relay_up_b, span, near_below, lands_below),
        (cross_down, -span, low, 2, relay_up_b, span - 1, near_above, lands_above),
        (cross_down, span - 1, high, 3, relay_up_a, -span, near_above, lands_above),
    ]
    for start, first_hop, levels, slot, relays, second_hop, target, lands in routes:
        for piece in range(pieces):
            part = pl.ds(piece * (rows // pieces), rows // pieces)
            plan.append((start, first_hop, x_ref.at[part, levels], relay_ref.at[slot, part], relays))
            feeds[len(plan)] = len(plan) - 1
            plan.append((relays, second_hop, relay_ref.at[slot, part], target.at[part, levels], lands))

    barrier = pltpu.get_barrier_semaphore()
    offsets = sorted({entry[1] for entry in plan})
    for offset in offsets:
        neighbour = lax.rem(here + offset + count, count)
        pl.semaphore_signal(barrier, 1, device_id=(neighbour, column), device_id_type=mesh)
    pl.semaphore_wait(barrier, len(offsets))

    def copy(slot, device):
        _, _, src, dst, _ = plan[slot]
        return pltpu.make_async_remote_copy(
            src_ref=src, dst_ref=dst, send_sem=send_sem.at[slot], recv_sem=recv_sem.at[slot],
            device_id=(device, column), device_id_type=mesh,
        )

    def when_start(slot):
        sends, offset, _, _, _ = plan[slot]

        @pl.when(sends)
        def _():
            copy(slot, here + offset).start()

    for slot in range(len(plan)):
        if slot not in feeds:
            when_start(slot)
    for slot, source in feeds.items():
        @pl.when(plan[slot][0])
        def _():
            copy(source, here).wait_recv()
            copy(slot, here + plan[slot][1]).start()
    for slot in range(len(plan)):
        sends, offset, _, _, receives = plan[slot]

        @pl.when(sends)
        def _():
            copy(slot, here + offset).wait_send()

        if slot in feeds.values():
            continue

        @pl.when(receives)
        def _():
            copy(slot, here).wait_recv()


def lat_halo_kernel(block, width, span):
    rows = block.shape[0]
    far = width - rows
    count = lax.axis_size("lat")
    halo_shape = jax.ShapeDtypeStruct((width,) + block.shape[1:], block.dtype)
    levels = block.shape[1]
    relay_shape = jax.ShapeDtypeStruct((4, rows, levels // 2, block.shape[2]), block.dtype)
    pieces = 3 if rows % 3 == 0 else 1
    slots = 4 + 8 * pieces
    below, above, _ = pl.pallas_call(
        functools.partial(relay_halo_body, count, span, pieces, rows, far),
        out_shape=(halo_shape, halo_shape, relay_shape),
        in_specs=[pl.BlockSpec(memory_space=pl.ANY)],
        out_specs=(pl.BlockSpec(memory_space=pl.ANY),) * 3,
        scratch_shapes=[pltpu.SemaphoreType.DMA((slots,)), pltpu.SemaphoreType.DMA((slots,))],
        compiler_params=pltpu.CompilerParams(collective_id=0, has_side_effects=True),
    )(block)
    here = lax.axis_index("lat")
    row = jnp.arange(width)[:, None, None]
    below = jnp.where(jnp.where(row >= far, here >= 1, here >= 2), below, 0.0)
    above = jnp.where(jnp.where(row < rows, here + 1 < count, here + 2 < count), above, 0.0)
    return jnp.concatenate([below, block, above], axis=0)


def shards(
    span,
    obs_values, obs_rows, obs_cols, row_frac, col_frac, obs_count, sigma, lat_scales, lon_scales
):
    tile_rows, level_count, tile_cols = sigma.shape
    slot_total = obs_rows.shape[0]
    live_slot = jnp.arange(slot_total, dtype=jnp.int32) < obs_count[0]
    values_t = jnp.where(live_slot[:, None], jnp.transpose(obs_values), 0.0)
    row_w = corner_weights(obs_rows, row_frac, tile_rows + 1)
    col_w = corner_weights(obs_cols, col_frac, tile_cols + 1)
    row_values = values_t[:, :, None] * row_w[:, None, :]
    extended = jnp.einsum(
        "klr,kc->rlc", row_values, col_w, precision=lax.Precision.HIGH
    )
    edge_column = from_behind(extended[:, :, tile_cols], "lon", 1)
    folded = jnp.concatenate(
        [(extended[:, :, 0] + edge_column)[:, :, None], extended[:, :, 1:tile_cols]], axis=2
    )
    edge_row = shifted(folded[tile_rows], "lat", 1)
    departures = jnp.concatenate([(folded[0] + edge_row)[None], folded[1:tile_rows]], axis=0)
    weighted = departures * sigma
    half_width = HALF
    window = lat_halo_kernel(weighted, half_width, span)
    lat_kernel = kernel_matrix(lat_scales, tile_rows, half_width)
    lat_done = jnp.einsum(
        "lip,plc->ilc", lat_kernel, window, precision=lax.Precision.HIGH
    )
    padded_cols = with_halo(lat_done, (("lon", 2),), half_width)
    band = half_width
    lon_kernel = kernel_matrix(lon_scales, band, half_width)
    band_count = tile_cols // band
    bands = jnp.stack(
        [padded_cols[:, :, b * band : b * band + band + 2 * half_width] for b in range(band_count)],
        axis=2,
    )
    result = jnp.einsum("lip,rlbp->rlbi", lon_kernel, bands, precision=lax.Precision.HIGH)
    return result.reshape(tile_rows, level_count, tile_cols)


def lat_groups(mesh):
    column = mesh.devices[:, 0]
    coords = [getattr(device, "coords", None) for device in column]
    if any(c is None for c in coords):
        return tuple(index // 8 for index in range(len(column)))
    return tuple(c[2] // 2 for c in coords)


def solution(mesh):
    in_specs = (
        P(None, ("lat", "lon")),
        P(("lat", "lon")),
        P(("lat", "lon")),
        P(("lat", "lon")),
        P(("lat", "lon")),
        P(("lat", "lon")),
        P("lat", None, "lon"),
        P(),
        P(),
    )
    out_specs = P("lat", None, "lon")
    groups = lat_groups(mesh)
    span = groups.index(groups[0] + 1) if groups[0] + 1 in groups else len(groups)
    return jax.shard_map(functools.partial(shards, span), mesh=mesh, in_specs=in_specs, out_specs=out_specs, check_vma=False)
```

```python
import functools

import jax
import jax.numpy as jnp
from jax import lax
from jax.experimental import pallas as pl
from jax.experimental.pallas import tpu as pltpu
from jax.sharding import PartitionSpec as P

HALF = 128


def from_behind(block, axis, distance):
    devices = range(lax.axis_size(axis))
    route = [((i - distance) % len(devices), i) for i in devices]
    return lax.ppermute(block, axis, route)


def shifted(block, axis, distance):
    devices = range(lax.axis_size(axis))
    route = [(i - distance, i) for i in devices if i - distance in devices]
    return lax.ppermute(block, axis, route)


def with_halo(block, sides, width):
    for axis, dim in sides:
        count = lax.axis_size(axis)
        forward = [(i, i + 1) for i in range(count - 1)]
        forward.append((count - 1, 0))
        backward = [(target, source) for source, target in forward]
        low = lax.ppermute(
            lax.slice_in_dim(block, block.shape[dim] - width, None, axis=dim), axis, forward
        )
        high = lax.ppermute(lax.slice_in_dim(block, 0, width, axis=dim), axis, backward)
        block = jnp.concatenate([low, block, high], axis=dim)
    return block


def kernel_matrix(scales, out_count, half_width):
    out_index = jnp.arange(out_count, dtype=jnp.int32)[:, None]
    in_index = jnp.arange(out_count + 2 * half_width, dtype=jnp.int32)[None, :]
    offset = in_index - half_width - out_index
    inside = jnp.abs(offset) <= half_width
    offset_real = offset.astype(jnp.float32)
    spread = scales[:, None, None]
    tap_lag = jnp.arange(-half_width, half_width + 1, dtype=jnp.int32).astype(jnp.float32)
    energy = jnp.sum(
        jnp.exp(-(tap_lag[None, :] * tap_lag[None, :]) / (spread[:, :, 0] * spread[:, :, 0])),
        axis=1,
    )
    gaussian = (
        jnp.exp(-(offset_real * offset_real)[None] / (2.0 * spread * spread))
        / jnp.sqrt(energy)[:, None, None]
    )
    return jnp.where(inside[None], gaussian, jnp.zeros_like(gaussian))


def corner_weights(index, frac, count):
    cells = jnp.arange(count, dtype=jnp.int32)[None, :]
    low = jnp.where(cells == index[:, None], (1.0 - frac)[:, None], 0.0)
    high = jnp.where(cells == index[:, None] + 1, frac[:, None], 0.0)
    return low + high


def lat_halo(block, width):
    rows = block.shape[0]
    parts = []
    reach = width
    distance = 1
    below, above = [], []
    while reach > 0:
        take = min(rows, reach)
        below.insert(0, shifted(block[rows - take :], "lat", distance))
        above.append(shifted(block[:take], "lat", -distance))
        reach -= take
        distance += 1
    parts = below + [block] + above
    return jnp.concatenate(parts, axis=0)


def relay_halo_body(count, span, pieces, rows, far, x_ref, below_ref, above_ref, relay_ref, send_sem, recv_sem):
    here = lax.axis_index("lat")
    column = lax.axis_index("lon")
    mesh = pl.DeviceIdType.MESH
    half = x_ref.shape[1] // 2
    last = span - 1
    first_of = here % span == 0
    last_of = here % span == last
    up_exists = here + 1 < count
    down_exists = here >= 1
    cross_up = jnp.logical_and(up_exists, (here + 1) % span == 0)
    cross_down = jnp.logical_and(down_exists, first_of)
    low, high = pl.ds(0, half), pl.ds(half, half)
    near_below = below_ref.at[pl.ds(far, rows)]
    near_above = above_ref.at[pl.ds(0, rows)]
    plan = [
        (here + 2 < count, 2, x_ref.at[pl.ds(rows - far, far)], below_ref.at[pl.ds(0, far)], here >= 2),
        (here >= 2, -2, x_ref.at[pl.ds(0, far)], above_ref.at[pl.ds(rows, far)], here + 2 < count),
        (jnp.logical_and(up_exists, jnp.logical_not(cross_up)), 1, x_ref, near_below,
         jnp.logical_and(down_exists, jnp.logical_not(first_of))),
        (jnp.logical_and(down_exists, jnp.logical_not(first_of)), -1, x_ref, near_above,
         jnp.logical_and(up_exists, jnp.logical_not(cross_up))),
    ]
    feeds = {}
    relay_up_a = jnp.logical_and(last_of, here >= span)
    relay_up_b = jnp.logical_and(first_of, here + span < count)
    lands_below = jnp.logical_and(first_of, here >= span)
    lands_above = jnp.logical_and(last_of, up_exists)
    routes = [
        (cross_up, span, low, 0, relay_up_a, 1 - span, near_below, lands_below),
        (cross_up, 1 - span, high, 1, relay_up_b, span, near_below, lands_below),
        (cross_down, -span, low, 2, relay_up_b, span - 1, near_above, lands_above),
        (cross_down, span - 1, high, 3, relay_up_a, -span, near_above, lands_above),
    ]
    for start, first_hop, levels, slot, relays, second_hop, target, lands in routes:
        for piece in range(pieces):
            part = pl.ds(piece * (rows // pieces), rows // pieces)
            plan.append((start, first_hop, x_ref.at[part, levels], relay_ref.at[slot, part], relays))
            feeds[len(plan)] = len(plan) - 1
            plan.append((relays, second_hop, relay_ref.at[slot, part], target.at[part, levels], lands))

    barrier = pltpu.get_barrier_semaphore()
    offsets = sorted({entry[1] for entry in plan})
    for offset in offsets:
        neighbour = lax.rem(here + offset + count, count)
        pl.semaphore_signal(barrier, 1, device_id=(neighbour, column), device_id_type=mesh)
    pl.semaphore_wait(barrier, len(offsets))

    def copy(slot, device):
        _, _, src, dst, _ = plan[slot]
        return pltpu.make_async_remote_copy(
            src_ref=src, dst_ref=dst, send_sem=send_sem.at[slot], recv_sem=recv_sem.at[slot],
            device_id=(device, column), device_id_type=mesh,
        )

    def when_start(slot):
        sends, offset, _, _, _ = plan[slot]

        @pl.when(sends)
        def _():
            copy(slot, here + offset).start()

    for slot in range(len(plan)):
        if slot not in feeds:
            when_start(slot)
    for slot, source in feeds.items():
        @pl.when(plan[slot][0])
        def _():
            copy(source, here).wait_recv()
            copy(slot, here + plan[slot][1]).start()
    for slot in range(len(plan)):
        sends, offset, _, _, receives = plan[slot]

        @pl.when(sends)
        def _():
            copy(slot, here + offset).wait_send()

        if slot in feeds.values():
            continue

        @pl.when(receives)
        def _():
            copy(slot, here).wait_recv()


def lat_halo_kernel(block, width, span):
    rows = block.shape[0]
    far = width - rows
    count = lax.axis_size("lat")
    halo_shape = jax.ShapeDtypeStruct((width,) + block.shape[1:], block.dtype)
    levels = block.shape[1]
    relay_shape = jax.ShapeDtypeStruct((4, rows, levels // 2, block.shape[2]), block.dtype)
    pieces = 4 if rows % 4 == 0 else 1
    slots = 4 + 8 * pieces
    below, above, _ = pl.pallas_call(
        functools.partial(relay_halo_body, count, span, pieces, rows, far),
        out_shape=(halo_shape, halo_shape, relay_shape),
        in_specs=[pl.BlockSpec(memory_space=pl.ANY)],
        out_specs=(pl.BlockSpec(memory_space=pl.ANY),) * 3,
        scratch_shapes=[pltpu.SemaphoreType.DMA((slots,)), pltpu.SemaphoreType.DMA((slots,))],
        compiler_params=pltpu.CompilerParams(collective_id=0, has_side_effects=True),
    )(block)
    here = lax.axis_index("lat")
    row = jnp.arange(width)[:, None, None]
    below = jnp.where(jnp.where(row >= far, here >= 1, here >= 2), below, 0.0)
    above = jnp.where(jnp.where(row < rows, here + 1 < count, here + 2 < count), above, 0.0)
    return jnp.concatenate([below, block, above], axis=0)


def shards(
    span,
    obs_values, obs_rows, obs_cols, row_frac, col_frac, obs_count, sigma, lat_scales, lon_scales
):
    tile_rows, level_count, tile_cols = sigma.shape
    slot_total = obs_rows.shape[0]
    live_slot = jnp.arange(slot_total, dtype=jnp.int32) < obs_count[0]
    values_t = jnp.where(live_slot[:, None], jnp.transpose(obs_values), 0.0)
    row_w = corner_weights(obs_rows, row_frac, tile_rows + 1)
    col_w = corner_weights(obs_cols, col_frac, tile_cols + 1)
    row_values = values_t[:, :, None] * row_w[:, None, :]
    extended = jnp.einsum(
        "klr,kc->rlc", row_values, col_w, precision=lax.Precision.HIGH
    )
    edge_column = from_behind(extended[:, :, tile_cols], "lon", 1)
    folded = jnp.concatenate(
        [(extended[:, :, 0] + edge_column)[:, :, None], extended[:, :, 1:tile_cols]], axis=2
    )
    edge_row = shifted(folded[tile_rows], "lat", 1)
    departures = jnp.concatenate([(folded[0] + edge_row)[None], folded[1:tile_rows]], axis=0)
    weighted = departures * sigma
    half_width = HALF
    window = lat_halo_kernel(weighted, half_width, span)
    lat_kernel = kernel_matrix(lat_scales, tile_rows, half_width)
    lat_done = jnp.einsum(
        "lip,plc->ilc", lat_kernel, window, precision=lax.Precision.HIGH
    )
    padded_cols = with_halo(lat_done, (("lon", 2),), half_width)
    band = half_width
    lon_kernel = kernel_matrix(lon_scales, band, half_width)
    band_count = tile_cols // band
    bands = jnp.stack(
        [padded_cols[:, :, b * band : b * band + band + 2 * half_width] for b in range(band_count)],
        axis=2,
    )
    result = jnp.einsum("lip,rlbp->rlbi", lon_kernel, bands, precision=lax.Precision.HIGH)
    return result.reshape(tile_rows, level_count, tile_cols)


def lat_groups(mesh):
    column = mesh.devices[:, 0]
    coords = [getattr(device, "coords", None) for device in column]
    if any(c is None for c in coords):
        return tuple(index // 8 for index in range(len(column)))
    return tuple(c[2] // 2 for c in coords)


def solution(mesh):
    in_specs = (
        P(None, ("lat", "lon")),
        P(("lat", "lon")),
        P(("lat", "lon")),
        P(("lat", "lon")),
        P(("lat", "lon")),
        P(("lat", "lon")),
        P("lat", None, "lon"),
        P(),
        P(),
    )
    out_specs = P("lat", None, "lon")
    groups = lat_groups(mesh)
    span = groups.index(groups[0] + 1) if groups[0] + 1 in groups else len(groups)
    return jax.shard_map(functools.partial(shards, span), mesh=mesh, in_specs=in_specs, out_specs=out_specs, check_vma=False)
```

```python
import functools

import jax
import jax.numpy as jnp
from jax import lax
from jax.experimental import pallas as pl
from jax.experimental.pallas import tpu as pltpu
from jax.sharding import PartitionSpec as P

HALF = 128


def from_behind(block, axis, distance):
    devices = range(lax.axis_size(axis))
    route = [((i - distance) % len(devices), i) for i in devices]
    return lax.ppermute(block, axis, route)


def shifted(block, axis, distance):
    devices = range(lax.axis_size(axis))
    route = [(i - distance, i) for i in devices if i - distance in devices]
    return lax.ppermute(block, axis, route)


def with_halo(block, sides, width):
    for axis, dim in sides:
        count = lax.axis_size(axis)
        forward = [(i, i + 1) for i in range(count - 1)]
        forward.append((count - 1, 0))
        backward = [(target, source) for source, target in forward]
        low = lax.ppermute(
            lax.slice_in_dim(block, block.shape[dim] - width, None, axis=dim), axis, forward
        )
        high = lax.ppermute(lax.slice_in_dim(block, 0, width, axis=dim), axis, backward)
        block = jnp.concatenate([low, block, high], axis=dim)
    return block


def kernel_matrix(scales, out_count, half_width):
    out_index = jnp.arange(out_count, dtype=jnp.int32)[:, None]
    in_index = jnp.arange(out_count + 2 * half_width, dtype=jnp.int32)[None, :]
    offset = in_index - half_width - out_index
    inside = jnp.abs(offset) <= half_width
    offset_real = offset.astype(jnp.float32)
    spread = scales[:, None, None]
    tap_lag = jnp.arange(-half_width, half_width + 1, dtype=jnp.int32).astype(jnp.float32)
    energy = jnp.sum(
        jnp.exp(-(tap_lag[None, :] * tap_lag[None, :]) / (spread[:, :, 0] * spread[:, :, 0])),
        axis=1,
    )
    gaussian = (
        jnp.exp(-(offset_real * offset_real)[None] / (2.0 * spread * spread))
        / jnp.sqrt(energy)[:, None, None]
    )
    return jnp.where(inside[None], gaussian, jnp.zeros_like(gaussian))


def corner_weights(index, frac, count):
    cells = jnp.arange(count, dtype=jnp.int32)[None, :]
    low = jnp.where(cells == index[:, None], (1.0 - frac)[:, None], 0.0)
    high = jnp.where(cells == index[:, None] + 1, frac[:, None], 0.0)
    return low + high


def lat_halo(block, width):
    rows = block.shape[0]
    parts = []
    reach = width
    distance = 1
    below, above = [], []
    while reach > 0:
        take = min(rows, reach)
        below.insert(0, shifted(block[rows - take :], "lat", distance))
        above.append(shifted(block[:take], "lat", -distance))
        reach -= take
        distance += 1
    parts = below + [block] + above
    return jnp.concatenate(parts, axis=0)


def relay_halo_body(count, span, pieces, rows, far, x_ref, below_ref, above_ref, relay_ref, send_sem, recv_sem):
    here = lax.axis_index("lat")
    column = lax.axis_index("lon")
    mesh = pl.DeviceIdType.MESH
    half = x_ref.shape[1] // 2
    last = span - 1
    first_of = here % span == 0
    last_of = here % span == last
    up_exists = here + 1 < count
    down_exists = here >= 1
    cross_up = jnp.logical_and(up_exists, (here + 1) % span == 0)
    cross_down = jnp.logical_and(down_exists, first_of)
    low, high = pl.ds(0, half), pl.ds(half, half)
    near_below = below_ref.at[pl.ds(far, rows)]
    near_above = above_ref.at[pl.ds(0, rows)]
    plan = [
        (jnp.logical_and(here + 2 < count, here % span < span - 2), 2, x_ref.at[pl.ds(rows - far, far)],
         below_ref.at[pl.ds(0, far)], jnp.logical_and(here >= 2, here % span >= 2)),
        (jnp.logical_and(here >= 2, here % span >= 2), -2, x_ref.at[pl.ds(0, far)],
         above_ref.at[pl.ds(rows, far)], jnp.logical_and(here + 2 < count, here % span < span - 2)),
        (jnp.logical_and(up_exists, jnp.logical_not(cross_up)), 1, x_ref, near_below,
         jnp.logical_and(down_exists, jnp.logical_not(first_of))),
        (jnp.logical_and(down_exists, jnp.logical_not(first_of)), -1, x_ref, near_above,
         jnp.logical_and(up_exists, jnp.logical_not(cross_up))),
    ]
    feeds = {}
    relay_up_a = jnp.logical_and(last_of, here >= span)
    relay_up_b = jnp.logical_and(first_of, here + span < count)
    lands_below = jnp.logical_and(first_of, here >= span)
    lands_above = jnp.logical_and(last_of, up_exists)
    routes = [
        (cross_up, span, low, 0, relay_up_a, 1 - span, near_below, lands_below),
        (cross_up, 1 - span, high, 1, relay_up_b, span, near_below, lands_below),
        (cross_down, -span, low, 2, relay_up_b, span - 1, near_above, lands_above),
        (cross_down, span - 1, high, 3, relay_up_a, -span, near_above, lands_above),
    ]
    for start, first_hop, levels, slot, relays, second_hop, target, lands in routes:
        for piece in range(pieces):
            part = pl.ds(piece * (rows // pieces), rows // pieces)
            plan.append((start, first_hop, x_ref.at[part, levels], relay_ref.at[slot, part], relays))
            feeds[len(plan)] = len(plan) - 1
            plan.append((relays, second_hop, relay_ref.at[slot, part], target.at[part, levels], lands))
    top_rows = x_ref.at[pl.ds(rows - far, far)]
    bottom_rows = x_ref.at[pl.ds(0, far)]
    edge = pl.ds(0, far)
    for lane in (span - 2, span - 1):
        up_start = jnp.logical_and(here % span == lane, here + 2 < count)
        up_a = jnp.logical_and(here % span == lane, here >= span)
        up_b = jnp.logical_and(here % span == lane + 2 - span, here + span < count)
        up_lands = jnp.logical_and(here % span == lane + 2 - span, here >= span)
        down_start = jnp.logical_and(here % span == lane + 2 - span, here >= span)
        down_lands = jnp.logical_and(here % span == lane, here + 2 < count)
        far_routes = [
            (up_start, span, top_rows.at[:, low], 4, up_a, 2 - span, below_ref.at[edge, low], up_lands),
            (up_start, 2 - span, top_rows.at[:, high], 5, up_b, span, below_ref.at[edge, high], up_lands),
            (down_start, -span, bottom_rows.at[:, low], 6, up_b, span - 2,
             above_ref.at[pl.ds(rows, far), low], down_lands),
            (down_start, span - 2, bottom_rows.at[:, high], 7, up_a, -span,
             above_ref.at[pl.ds(rows, far), high], down_lands),
        ]
        for start, first_hop, source, slot, relays, second_hop, target, lands in far_routes:
            held = relay_ref.at[slot, pl.ds((lane - span + 2) * far, far)]
            plan.append((start, first_hop, source, held, relays))
            feeds[len(plan)] = len(plan) - 1
            plan.append((relays, second_hop, held, target, lands))

    barrier = pltpu.get_barrier_semaphore()
    offsets = sorted({entry[1] for entry in plan})
    for offset in offsets:
        neighbour = lax.rem(here + offset + count, count)
        pl.semaphore_signal(barrier, 1, device_id=(neighbour, column), device_id_type=mesh)
    pl.semaphore_wait(barrier, len(offsets))

    def copy(slot, device):
        _, _, src, dst, _ = plan[slot]
        return pltpu.make_async_remote_copy(
            src_ref=src, dst_ref=dst, send_sem=send_sem.at[slot], recv_sem=recv_sem.at[slot],
            device_id=(device, column), device_id_type=mesh,
        )

    def when_start(slot):
        sends, offset, _, _, _ = plan[slot]

        @pl.when(sends)
        def _():
            copy(slot, here + offset).start()

    for slot in range(len(plan)):
        if slot not in feeds:
            when_start(slot)
    for slot, source in feeds.items():
        @pl.when(plan[slot][0])
        def _():
            copy(source, here).wait_recv()
            copy(slot, here + plan[slot][1]).start()
    for slot in range(len(plan)):
        sends, offset, _, _, receives = plan[slot]

        @pl.when(sends)
        def _():
            copy(slot, here + offset).wait_send()

        if slot in feeds.values():
            continue

        @pl.when(receives)
        def _():
            copy(slot, here).wait_recv()


def lat_halo_kernel(block, width, span):
    rows = block.shape[0]
    far = width - rows
    count = lax.axis_size("lat")
    halo_shape = jax.ShapeDtypeStruct((width,) + block.shape[1:], block.dtype)
    levels = block.shape[1]
    relay_shape = jax.ShapeDtypeStruct((8, rows, levels // 2, block.shape[2]), block.dtype)
    pieces = 3 if rows % 3 == 0 else 1
    slots = 4 + 8 * pieces + 16
    below, above, _ = pl.pallas_call(
        functools.partial(relay_halo_body, count, span, pieces, rows, far),
        out_shape=(halo_shape, halo_shape, relay_shape),
        in_specs=[pl.BlockSpec(memory_space=pl.ANY)],
        out_specs=(pl.BlockSpec(memory_space=pl.ANY),) * 3,
        scratch_shapes=[pltpu.SemaphoreType.DMA((slots,)), pltpu.SemaphoreType.DMA((slots,))],
        compiler_params=pltpu.CompilerParams(collective_id=0, has_side_effects=True),
    )(block)
    here = lax.axis_index("lat")
    row = jnp.arange(width)[:, None, None]
    below = jnp.where(jnp.where(row >= far, here >= 1, here >= 2), below, 0.0)
    above = jnp.where(jnp.where(row < rows, here + 1 < count, here + 2 < count), above, 0.0)
    return jnp.concatenate([below, block, above], axis=0)


def shards(
    span,
    obs_values, obs_rows, obs_cols, row_frac, col_frac, obs_count, sigma, lat_scales, lon_scales
):
    tile_rows, level_count, tile_cols = sigma.shape
    slot_total = obs_rows.shape[0]
    live_slot = jnp.arange(slot_total, dtype=jnp.int32) < obs_count[0]
    values_t = jnp.where(live_slot[:, None], jnp.transpose(obs_values), 0.0)
    row_w = corner_weights(obs_rows, row_frac, tile_rows + 1)
    col_w = corner_weights(obs_cols, col_frac, tile_cols + 1)
    row_values = values_t[:, :, None] * row_w[:, None, :]
    extended = jnp.einsum(
        "klr,kc->rlc", row_values, col_w, precision=lax.Precision.HIGH
    )
    edge_column = from_behind(extended[:, :, tile_cols], "lon", 1)
    folded = jnp.concatenate(
        [(extended[:, :, 0] + edge_column)[:, :, None], extended[:, :, 1:tile_cols]], axis=2
    )
    edge_row = shifted(folded[tile_rows], "lat", 1)
    departures = jnp.concatenate([(folded[0] + edge_row)[None], folded[1:tile_rows]], axis=0)
    weighted = departures * sigma
    half_width = HALF
    window = lat_halo_kernel(weighted, half_width, span)
    lat_kernel = kernel_matrix(lat_scales, tile_rows, half_width)
    lat_done = jnp.einsum(
        "lip,plc->ilc", lat_kernel, window, precision=lax.Precision.HIGH
    )
    padded_cols = with_halo(lat_done, (("lon", 2),), half_width)
    band = half_width
    lon_kernel = kernel_matrix(lon_scales, band, half_width)
    band_count = tile_cols // band
    bands = jnp.stack(
        [padded_cols[:, :, b * band : b * band + band + 2 * half_width] for b in range(band_count)],
        axis=2,
    )
    result = jnp.einsum("lip,rlbp->rlbi", lon_kernel, bands, precision=lax.Precision.HIGH)
    return result.reshape(tile_rows, level_count, tile_cols)


def lat_groups(mesh):
    column = mesh.devices[:, 0]
    coords = [getattr(device, "coords", None) for device in column]
    if any(c is None for c in coords):
        return tuple(index // 8 for index in range(len(column)))
    return tuple(c[2] // 2 for c in coords)


def solution(mesh):
    in_specs = (
        P(None, ("lat", "lon")),
        P(("lat", "lon")),
        P(("lat", "lon")),
        P(("lat", "lon")),
        P(("lat", "lon")),
        P(("lat", "lon")),
        P("lat", None, "lon"),
        P(),
        P(),
    )
    out_specs = P("lat", None, "lon")
    groups = lat_groups(mesh)
    span = groups.index(groups[0] + 1) if groups[0] + 1 in groups else len(groups)
    return jax.shard_map(functools.partial(shards, span), mesh=mesh, in_specs=in_specs, out_specs=out_specs, check_vma=False)
```
